1024 devices in a mesh: rad: 64 (over y, z_lo, core), azi: 16 (over x, z_hi).
Axes of the slice: x: 4, y: 8, z: 16 (z_hi: 4, z_lo: 4; z = z_hi * 4 + z_lo), core: 2. Of those that a mesh axis runs over, the one named last changes fastest.
Arguments:
- state: float32 [5, 4, 1024, 2048], P(None, None, 'rad', 'azi'), may hold values from -6 to 6
- shifts: int32 [1024], replicated, may hold values from 0 to 2047
- spin: float32 [1024], replicated, may hold values from 0.2 to 1
- drift: float32 [1024], replicated, may hold values from -1.5 to 1.5
- stiffness: float32 [4, 1024], replicated, may hold values from 0.5 to 2
Outputs:
- evolved: float32 [5, 4, 1024, 2048], P(None, None, 'rad', 'azi')
The draws below stay inside these ranges and needn't reach their ends.
All inputs are finite; a program needn't handle non-finite values.
Results may differ from the reference program's by a relative error of at most 0.00002.
Values sent between devices are 32-bit elements; how exact they have to be, the bound alone decides.
No kernel may reach another device: no remote copies, remote signals or barrier semaphores. Data moves between devices by JAX's collectives and lax.ppermute only.
A program may use at most 32 MiB of HBM per device.

```python
import math
import jax
import jax.numpy as jnp

NV = 4
STEPS = 2
NR = 1024
NA = 2048


def plant(array, own_key, smallest, top_value):
    longest = array.shape.index(max(array.shape))
    spots = []
    for shift in (0, 1):
        where = [jax.random.randint(jax.random.fold_in(own_key, axis), (), 0, length) for axis, length in enumerate(array.shape)]
        where[longest] = (where[longest] + shift) % array.shape[longest]
        spots.append(tuple(where))
    return array.at[spots[0]].set(smallest).at[spots[1]].set(top_value)


def level_of(stream_key, shape, pieces, least, top_value):
    level = 1.0
    for dim, shards_of in pieces:
        heights = jax.random.uniform(jax.random.fold_in(jax.random.fold_in(stream_key, 6), dim), (shards_of,), jnp.float32, least / len(pieces), top_value / len(pieces))
        level = level * jnp.repeat(jnp.exp(heights), shape[dim] // shards_of).reshape((-1,) + (1,) * (len(shape) - 1 - dim))
    return level


def normal_values(own_key, extent, spread, reach, shards=(), kind=jnp.bfloat16):
    values = spread * jax.random.normal(own_key, extent, jnp.float32)
    if shards:
        values = values * level_of(own_key, extent, shards, -0.22, 0.18)
    return jnp.clip(values, -reach, reach).astype(kind)


def setup_inputs(seed: int = 0) -> dict:
    keys = jax.random.split(jax.random.key(seed), 6)
    state = normal_values(keys[0], (5, NV, NR, NA), 1.0, 6.0, ((2, 64), (3, 16)), jnp.float32)
    shifts = plant(jax.random.randint(keys[1], (NR,), 0, NA), jax.random.fold_in(keys[1], 1), 0, NA - 1).astype(jnp.int32)
    spin = jnp.clip(jnp.exp(jax.random.uniform(keys[2], (NR,), jnp.float32, math.log(0.2), math.log(1.0))), 0.2, 1.0)
    drift = jnp.clip(jax.random.uniform(keys[3], (NR,), jnp.float32, -1.5, 1.5), -1.5, 1.5)
    stiffness = jnp.clip(jnp.exp(jax.random.uniform(keys[4], (NV, NR), jnp.float32, math.log(0.5), math.log(2.0))), 0.5, 2.0)
    return dict(state=state, shifts=shifts, spin=spin, drift=drift, stiffness=stiffness)


time_step = 0.15
diffuse = 0.05


def tendency(extended, stiff_rows, spin_rows, drift_rows):
    centre_cells = extended[:, :, 1:-1, 1:-1]
    upper_row = extended[:, :, 2:, 1:-1]
    lower_row = extended[:, :, :-2, 1:-1]
    ahead_cell = extended[:, :, 1:-1, 2:]
    behind_cell = extended[:, :, 1:-1, :-2]
    rad_slope = 0.5 * (upper_row - lower_row)
    azi_slope = 0.5 * (ahead_cell - behind_cell)
    laplace_sum = upper_row + lower_row + ahead_cell + behind_cell - 4.0 * centre_cells
    vertical_pad = jnp.pad(centre_cells[3:5], ((0, 0), (1, 1), (0, 0), (0, 0)))
    ver_slope = 0.5 * (vertical_pad[:, 2:] - vertical_pad[:, :-2])
    spin_col = spin_rows[:, None]
    drift_col = drift_rows[:, None]
    divergence = rad_slope[1] + azi_slope[2] + ver_slope[0]
    coupled = jnp.stack([
        -divergence,
        2.0 * spin_col * centre_cells[2] - rad_slope[4],
        -0.5 * spin_col * centre_cells[1] - azi_slope[4],
        -ver_slope[1],
        -stiff_rows[:, :, None] * divergence,
    ])
    return coupled - drift_col * azi_slope + diffuse * laplace_sum


def extend_grid(field):
    padded = jnp.pad(field, ((0, 0), (0, 0), (1, 1), (0, 0)))
    return jnp.concatenate([padded[..., -1:], padded, padded[..., :1]], axis=3)


def rotate_rows(field, shifts):
    total = field.shape[3]
    source_index = (jnp.arange(total, dtype=jnp.int32)[None, :] - shifts[:, None]) % total
    merged = field.reshape(-1, field.shape[2], total)
    moved = jax.vmap(lambda plane: jnp.take_along_axis(plane, source_index, axis=1))(merged)
    return moved.reshape(field.shape)


def reference(state, shifts, spin, drift, stiffness):
    current = state
    for step_index in range(STEPS):
        first = current + time_step * tendency(extend_grid(current), stiffness, spin, drift)
        second = 0.75 * current + 0.25 * (first + time_step * tendency(extend_grid(first), stiffness, spin, drift))
        sectioned = current / 3.0 + (2.0 / 3.0) * (second + time_step * tendency(extend_grid(second), stiffness, spin, drift))
        current = rotate_rows(sectioned, shifts)
    return current
```

```python
import jax
import jax.numpy as jnp
from jax import lax
from jax.experimental import pallas as pl
from jax.experimental.pallas import tpu as pltpu
from jax.sharding import PartitionSpec as P

STEPS = 2
DT = 0.15
HD = 0.5 * DT
NEAR = DT * 0.05
SELF = 4.0 * DT * 0.05

FIELDS = 5
LEVELS = 4
PLANES = FIELDS * LEVELS
ROWS = 16
LANES = 128
REACH = 3
HALO = 2 * REACH
TALL = 32
PACK = 24


def put_together(main, below, above, all_ref, edge_ref):
    lane = lax.broadcasted_iota(jnp.int32, (TALL, LANES), 1)
    edge = jnp.zeros((TALL, LANES), jnp.float32)
    for plane in range(PLANES):
        f, k = divmod(plane, LEVELS)
        all_ref[plane, 0:ROWS, :] = main[f, k]
        all_ref[plane, ROWS : ROWS + HALO, :] = below[f, k]
        all_ref[plane, ROWS + HALO : TALL - HALO, :] = jnp.zeros(
            (TALL - ROWS - 2 * HALO, LANES), jnp.float32
        )
        all_ref[plane, TALL - HALO : TALL, :] = above[f, k]
    for plane in range(PLANES):
        cells = all_ref[plane]
        if plane:
            cells = pltpu.roll(cells, HALO * plane, 1)
        here = (lane >= HALO * plane) & (lane < HALO * (plane + 1))
        edge = jnp.where(here, cells, edge)
    edge_ref[...] = edge


def advance(at, slopes, coefs):
    a1, a2, twice, half, stiff = coefs
    rho, u, v, w, p = [slopes(f) for f in range(FIELDS)]
    w_up, w_down, p_up, p_down = at
    g = (u[1] - u[2]) + (v[3] - v[4])
    if w_up is not None:
        g = g + w_up
    if w_down is not None:
        g = g - w_down
    g = HD * g
    lift = 0.0
    if p_up is not None:
        lift = lift + p_up
    if p_down is not None:
        lift = lift - p_down
    own = [
        -g,
        twice * v[0] - HD * (p[1] - p[2]),
        -(half * u[0]) - HD * (p[3] - p[4]),
        -HD * lift,
        -(stiff * g),
    ]
    return [
        extra + ((a1 * q[3] + a2 * q[4]) + (NEAR * (q[1] + q[2]) - SELF * q[0]))
        for extra, q in zip(own, (rho, u, v, w, p))
    ]


def combine(stage, start, now, change):
    if stage == 0:
        return now + change
    if stage == 1:
        return 0.75 * start + 0.25 * (now + change)
    return start * (1.0 / 3.0) + (2.0 / 3.0) * (now + change)


def first_step(all_ref, edge_ref, coef_ref, send_ref, begin, one, two, table):
    wide = 2 * LANES
    edge = edge_ref[...]
    for plane in range(PLANES):
        begin[plane, :, 0:LANES] = all_ref[plane]
        begin[plane, :, LANES:wide] = (
            pltpu.roll(edge, LANES - HALO * plane, 1) if plane else edge
        )

    def coef(i):
        part = coef_ref[i]
        return jnp.concatenate([part, part], axis=1)

    sources = (begin, one, two)
    targets = (one, two, None)
    lane = lax.broadcasted_iota(jnp.int32, (TALL, LANES), 1)
    for stage in range(3):
        src, dst = sources[stage], targets[stage]
        for k in range(LEVELS):

            def slopes(f):
                c = src[f * LEVELS + k]
                return (
                    c,
                    pltpu.roll(c, TALL - 1, 0),
                    pltpu.roll(c, 1, 0),
                    pltpu.roll(c, wide - 1, 1),
                    pltpu.roll(c, 1, 1),
                )

            at = (
                src[3 * LEVELS + k + 1] if k + 1 < LEVELS else None,
                src[3 * LEVELS + k - 1] if k else None,
                src[4 * LEVELS + k + 1] if k + 1 < LEVELS else None,
                src[4 * LEVELS + k - 1] if k else None,
            )
            coefs = (coef(0), coef(1), coef(2), coef(3), coef(4 + k))
            valid = coef(4 + LEVELS) > 0.5
            change = advance(at, slopes, coefs)
            for f in range(FIELDS):
                plane = f * LEVELS + k
                value = combine(stage, begin[plane], src[plane], change[f])
                value = jnp.where(valid, value, 0.0)
                if dst is not None:
                    dst[plane] = value
                else:
                    left = pltpu.roll(value[:, 0:LANES], LANES - REACH, 1)
                    right = pltpu.roll(value[:, LANES:wide], LANES - REACH, 1)
                    shown = jnp.where(lane < LANES - REACH, left, right)
                    shown = pltpu.roll(shown, REACH, 0)
                    table[pl.ds(plane, PACK, PLANES), :] = shown[0:PACK]
    size = (4 + HALO) * PLANES
    for group in range(4):
        send_ref[group] = table[group * 4 * PLANES : group * 4 * PLANES + size]


def spread(got_ref, send_ref):
    size = (1 + HALO) * PLANES
    for target in range(4):
        for z in range(4):
            send_ref[target, z] = got_ref[z, target * PLANES : target * PLANES + size]


def turned(cells, amount, lane):
    blocks = amount // LANES
    offset = amount % LANES
    cells = pltpu.roll(cells, offset, 1)
    near = pltpu.roll(cells, blocks, 0)
    far = pltpu.roll(cells, lax.rem(blocks + 1, 16), 0)
    return jnp.where(lane >= offset, near, far)


def second_step(amount_ref, coef_ref, got_ref, send_ref, begin, one, two):
    lane = lax.broadcasted_iota(jnp.int32, (16, LANES), 1)
    span = 1 + HALO
    for row in range(span):
        amount = amount_ref[row]
        for plane in range(PLANES):
            cells = got_ref[pl.ds(row * PLANES + plane, 16, span * PLANES), :]
            begin[row, plane] = turned(cells, amount, lane)

    sources = (begin, one, two)
    targets = (one, two, None)
    last_amount = amount_ref[span]
    for stage in range(3):
        src, dst = sources[stage], targets[stage]
        for row in range(stage + 1, span - 1 - stage):
            scalars = [coef_ref[row, i] for i in range(5 + LEVELS)]
            for k in range(LEVELS):

                def slopes(f):
                    plane = f * LEVELS + k
                    c = src[row, plane]
                    ahead = pltpu.roll(c, LANES - 1, 1)
                    ahead = jnp.where(
                        lane == LANES - 1, pltpu.roll(ahead, 15, 0), ahead
                    )
                    behind = pltpu.roll(c, 1, 1)
                    behind = jnp.where(lane == 0, pltpu.roll(behind, 1, 0), behind)
                    return c, src[row + 1, plane], src[row - 1, plane], ahead, behind

                at = (
                    src[row, 3 * LEVELS + k + 1] if k + 1 < LEVELS else None,
                    src[row, 3 * LEVELS + k - 1] if k else None,
                    src[row, 4 * LEVELS + k + 1] if k + 1 < LEVELS else None,
                    src[row, 4 * LEVELS + k - 1] if k else None,
                )
                coefs = tuple(scalars[0:4]) + (scalars[4 + k],)
                change = advance(at, slopes, coefs)
                for f in range(FIELDS):
                    plane = f * LEVELS + k
                    value = combine(stage, begin[row, plane], src[row, plane], change[f])
                    if row != REACH:
                        value = jnp.where(scalars[4 + LEVELS] > 0.5, value, 0.0)
                    if dst is not None:
                        dst[row, plane] = value
                    else:
                        send_ref[pl.ds(plane, 16, PACK), :] = turned(
                            value, last_amount, lane
                        )
    for j in range(16):
        send_ref[j * PACK + PLANES : (j + 1) * PACK, :] = jnp.zeros(
            (PACK - PLANES, LANES), jnp.float32
        )


def set_down(got_ref, out_ref):
    for plane in range(PLANES):
        f, k = divmod(plane, LEVELS)
        for z in range(4):
            out_ref[f, k, 4 * z : 4 * z + 4, :] = got_ref[
                pl.ds(z * PACK + plane, 4, 4 * PACK), :
            ]


VMEM = pl.BlockSpec(memory_space=pltpu.VMEM)
SMEM = pl.BlockSpec(memory_space=pltpu.SMEM)


def f32(*shape):
    return jax.ShapeDtypeStruct(shape, jnp.float32)


def call(body, out_shape, in_specs, scratch=()):
    many = isinstance(out_shape, tuple)
    return pl.pallas_call(
        body,
        name=body.__name__,
        out_shape=out_shape,
        in_specs=in_specs,
        out_specs=(VMEM,) * len(out_shape) if many else VMEM,
        scratch_shapes=list(scratch),
    )


def on_device(state, shifts, spin, drift, stiffness):
    rad = lax.axis_size("rad")
    azi = lax.axis_size("azi")
    ring = lax.axis_index("azi")
    total = spin.shape[0]
    row_start = lax.axis_index("rad") * ROWS

    below = lax.ppermute(
        state[:, :, 0:HALO, :], "rad", [(i + 1, i) for i in range(rad - 1)]
    )
    above = lax.ppermute(
        state[:, :, ROWS - HALO :, :], "rad", [(i, i + 1) for i in range(rad - 1)]
    )

    rows = jnp.concatenate(
        [
            jnp.stack(
                [
                    NEAR - HD * drift,
                    NEAR + HD * drift,
                    (2.0 * DT) * spin,
                    (0.5 * DT) * spin,
                ]
            ),
            stiffness,
            jnp.ones((1, total), jnp.float32),
        ],
        axis=0,
    )
    rows = jnp.pad(rows, ((0, 0), (HALO, HALO)))
    near = lax.dynamic_slice_in_dim(rows, row_start, ROWS + 2 * HALO, axis=1)
    near = jnp.concatenate(
        [
            near[:, HALO:],
            jnp.zeros((rows.shape[0], TALL - ROWS - 2 * HALO), jnp.float32),
            near[:, :HALO],
        ],
        axis=1,
    )
    near = jnp.broadcast_to(near[:, :, None], near.shape + (LANES,))

    own_row = row_start + 4 * (ring % 4) + ring // 4
    around = lax.dynamic_slice_in_dim(rows, own_row + REACH, 1 + HALO, axis=1).T
    turn = lax.dynamic_slice_in_dim(
        jnp.pad(shifts, (REACH, REACH)), own_row, 1 + HALO, axis=0
    )
    turn = jnp.concatenate([(turn + REACH) % (azi * LANES), turn[REACH : REACH + 1]])

    whole, edge = call(
        put_together, (f32(PLANES, TALL, LANES), f32(TALL, LANES)), [VMEM] * 3
    )(state, below, above)
    edge = lax.ppermute(edge, "azi", [((i + 1) % azi, i) for i in range(azi)])

    count = (4 + HALO) * PLANES
    tile = pltpu.VMEM((PLANES, TALL, 2 * LANES), jnp.float32)
    sent = call(
        first_step,
        f32(4, count, LANES),
        [VMEM] * 3,
        (tile, tile, tile, pltpu.VMEM((PACK * PLANES, LANES), jnp.float32)),
    )(whole, edge, near)
    along_z = [[4 * x + z for z in range(4)] for x in range(4)]
    along_x = [[4 * x + z for x in range(4)] for z in range(4)]
    got = lax.all_to_all(sent, "azi", 0, 0, axis_index_groups=along_z)
    size = (1 + HALO) * PLANES
    sent = call(spread, f32(4, 4, size, LANES), [VMEM])(got)
    got = lax.all_to_all(
        sent.reshape(4, 4 * size, LANES), "azi", 0, 0, axis_index_groups=along_x
    )
    band = pltpu.VMEM((1 + HALO, PLANES, 16, LANES), jnp.float32)
    sent = call(
        second_step, f32(16 * PACK, LANES), [SMEM, SMEM, VMEM], (band, band, band)
    )(turn, around, got.reshape(16 * size, LANES))
    got = lax.all_to_all(sent.reshape(16, PACK, LANES), "azi", 0, 0)
    return call(set_down, f32(FIELDS, LEVELS, ROWS, LANES), [VMEM])(
        got.reshape(16 * PACK, LANES)
    )


def solution(mesh):
    in_specs = (P(None, None, "rad", "azi"), P(), P(), P(), P())
    out_specs = P(None, None, "rad", "azi")
    return jax.shard_map(
        on_device, mesh=mesh, in_specs=in_specs, out_specs=out_specs, check_vma=False
    )
```

```python
import jax
import jax.numpy as jnp
from jax import lax
from jax.experimental import pallas as pl
from jax.experimental.pallas import tpu as pltpu
from jax.sharding import PartitionSpec as P

STEPS = 2
DT = 0.15
HD = 0.5 * DT
NEAR = DT * 0.05
SELF = 4.0 * DT * 0.05

FIELDS = 5
LEVELS = 4
PLANES = FIELDS * LEVELS
ROWS = 16
LANES = 128
REACH = 3
HALO = 2 * REACH
TALL = 32
PACK = 24
ROOM = 16 * 1024 * 1024


def put_together(main, below, above, all_ref, edge_ref):
    lane = lax.broadcasted_iota(jnp.int32, (TALL, LANES), 1)
    edge = jnp.zeros((TALL, LANES), jnp.float32)
    for plane in range(PLANES):
        f, k = divmod(plane, LEVELS)
        all_ref[plane, 0:ROWS, :] = main[f, k]
        all_ref[plane, ROWS : ROWS + HALO, :] = below[f, k]
        all_ref[plane, ROWS + HALO : TALL - HALO, :] = jnp.zeros(
            (TALL - ROWS - 2 * HALO, LANES), jnp.float32
        )
        all_ref[plane, TALL - HALO : TALL, :] = above[f, k]
    for plane in range(PLANES):
        cells = all_ref[plane]
        if plane:
            cells = pltpu.roll(cells, HALO * plane, 1)
        here = (lane >= HALO * plane) & (lane < HALO * (plane + 1))
        edge = jnp.where(here, cells, edge)
    edge_ref[...] = edge


def advance(at, slopes, coefs):
    a1, a2, twice, half, stiff = coefs
    rho, u, v, w, p = [slopes(f) for f in range(FIELDS)]
    w_up, w_down, p_up, p_down = at
    g = (u[1] - u[2]) + (v[3] - v[4])
    if w_up is not None:
        g = g + w_up
    if w_down is not None:
        g = g - w_down
    g = HD * g
    lift = 0.0
    if p_up is not None:
        lift = lift + p_up
    if p_down is not None:
        lift = lift - p_down
    own = [
        -g,
        twice * v[0] - HD * (p[1] - p[2]),
        -(half * u[0]) - HD * (p[3] - p[4]),
        -HD * lift,
        -(stiff * g),
    ]
    return [
        extra + ((a1 * q[3] + a2 * q[4]) + (NEAR * (q[1] + q[2]) - SELF * q[0]))
        for extra, q in zip(own, (rho, u, v, w, p))
    ]


def combine(stage, start, now, change):
    if stage == 0:
        return now + change
    if stage == 1:
        return 0.75 * start + 0.25 * (now + change)
    return start * (1.0 / 3.0) + (2.0 / 3.0) * (now + change)


def first_step(all_ref, edge_ref, row_ref, send_ref, begin, one, two, table, coef_ref):
    wide = 2 * LANES
    edge = edge_ref[...]
    for plane in range(PLANES):
        begin[plane, :, 0:LANES] = all_ref[plane]
        begin[plane, :, LANES:wide] = (
            pltpu.roll(edge, LANES - HALO * plane, 1) if plane else edge
        )

    for i in range(coef_ref.shape[0]):
        coef_ref[i] = jnp.broadcast_to(row_ref[:, i : i + 1], (TALL, LANES))

    def coef(i):
        part = coef_ref[i]
        return jnp.concatenate([part, part], axis=1)

    sources = (begin, one, two)
    targets = (one, two, None)
    lane = lax.broadcasted_iota(jnp.int32, (TALL, LANES), 1)
    for stage in range(3):
        src, dst = sources[stage], targets[stage]
        for k in range(LEVELS):

            def slopes(f):
                c = src[f * LEVELS + k]
                return (
                    c,
                    pltpu.roll(c, TALL - 1, 0),
                    pltpu.roll(c, 1, 0),
                    pltpu.roll(c, wide - 1, 1),
                    pltpu.roll(c, 1, 1),
                )

            at = (
                src[3 * LEVELS + k + 1] if k + 1 < LEVELS else None,
                src[3 * LEVELS + k - 1] if k else None,
                src[4 * LEVELS + k + 1] if k + 1 < LEVELS else None,
                src[4 * LEVELS + k - 1] if k else None,
            )
            coefs = (coef(0), coef(1), coef(2), coef(3), coef(4 + k))
            valid = coef(4 + LEVELS) > 0.5
            change = advance(at, slopes, coefs)
            for f in range(FIELDS):
                plane = f * LEVELS + k
                value = combine(stage, begin[plane], src[plane], change[f])
                value = jnp.where(valid, value, 0.0)
                if dst is not None:
                    dst[plane] = value
                else:
                    left = pltpu.roll(value[:, 0:LANES], LANES - REACH, 1)
                    right = pltpu.roll(value[:, LANES:wide], LANES - REACH, 1)
                    shown = jnp.where(lane < LANES - REACH, left, right)
                    shown = pltpu.roll(shown, REACH, 0)
                    table[pl.ds(plane, PACK, PLANES), :] = shown[0:PACK]
    size = (4 + HALO) * PLANES
    for group in range(4):
        send_ref[group] = table[group * 4 * PLANES : group * 4 * PLANES + size]


def spread(got_ref, send_ref):
    size = (1 + HALO) * PLANES
    for target in range(4):
        for z in range(4):
            send_ref[target, z * size : (z + 1) * size, :] = got_ref[
                z, target * PLANES : target * PLANES + size, :
            ]


def turned(cells, amount, lane):
    blocks = amount // LANES
    offset = amount % LANES
    cells = pltpu.roll(cells, offset, 1)
    near = pltpu.roll(cells, blocks, 0)
    far = pltpu.roll(cells, lax.rem(blocks + 1, 16), 0)
    return jnp.where(lane >= offset, near, far)


def second_step(amount_ref, coef_ref, got_ref, send_ref, begin, one, two):
    lane = lax.broadcasted_iota(jnp.int32, (16, LANES), 1)
    span = 1 + HALO
    for row in range(span):
        amount = amount_ref[row]
        for plane in range(PLANES):
            cells = got_ref[pl.ds(row * PLANES + plane, 16, span * PLANES), :]
            begin[row, plane] = turned(cells, amount, lane)

    sources = (begin, one, two)
    targets = (one, two, None)
    last_amount = amount_ref[span]
    for stage in range(3):
        src, dst = sources[stage], targets[stage]
        for row in range(stage + 1, span - 1 - stage):
            scalars = [coef_ref[row, i] for i in range(5 + LEVELS)]
            for k in range(LEVELS):

                def slopes(f):
                    plane = f * LEVELS + k
                    c = src[row, plane]
                    ahead = pltpu.roll(c, LANES - 1, 1)
                    ahead = jnp.where(
                        lane == LANES - 1, pltpu.roll(ahead, 15, 0), ahead
                    )
                    behind = pltpu.roll(c, 1, 1)
                    behind = jnp.where(lane == 0, pltpu.roll(behind, 1, 0), behind)
                    return c, src[row + 1, plane], src[row - 1, plane], ahead, behind

                at = (
                    src[row, 3 * LEVELS + k + 1] if k + 1 < LEVELS else None,
                    src[row, 3 * LEVELS + k - 1] if k else None,
                    src[row, 4 * LEVELS + k + 1] if k + 1 < LEVELS else None,
                    src[row, 4 * LEVELS + k - 1] if k else None,
                )
                coefs = tuple(scalars[0:4]) + (scalars[4 + k],)
                change = advance(at, slopes, coefs)
                for f in range(FIELDS):
                    plane = f * LEVELS + k
                    value = combine(stage, begin[row, plane], src[row, plane], change[f])
                    if row != REACH:
                        value = jnp.where(scalars[4 + LEVELS] > 0.5, value, 0.0)
                    if dst is not None:
                        dst[row, plane] = value
                    else:
                        send_ref[pl.ds(plane, 16, PACK), :] = turned(
                            value, last_amount, lane
                        )
    for j in range(16):
        send_ref[j * PACK + PLANES : (j + 1) * PACK, :] = jnp.zeros(
            (PACK - PLANES, LANES), jnp.float32
        )


def set_down(got_ref, out_ref):
    for plane in range(PLANES):
        f, k = divmod(plane, LEVELS)
        for z in range(4):
            out_ref[f, k, 4 * z : 4 * z + 4, :] = got_ref[
                pl.ds(z * PACK + plane, 4, 4 * PACK), :
            ]


VMEM = pl.BlockSpec(memory_space=pltpu.VMEM)
SMEM = pl.BlockSpec(memory_space=pltpu.SMEM)


def f32(*shape):
    return jax.ShapeDtypeStruct(shape, jnp.float32)


def call(body, out_shape, in_specs, scratch=()):
    many = isinstance(out_shape, tuple)
    return pl.pallas_call(
        body,
        name=body.__name__,
        out_shape=out_shape,
        in_specs=in_specs,
        out_specs=(VMEM,) * len(out_shape) if many else VMEM,
        scratch_shapes=list(scratch),
        compiler_params=pltpu.CompilerParams(vmem_limit_bytes=ROOM),
    )


def on_device(state, shifts, spin, drift, stiffness):
    rad = lax.axis_size("rad")
    azi = lax.axis_size("azi")
    ring = lax.axis_index("azi")
    total = spin.shape[0]
    row_start = lax.axis_index("rad") * ROWS

    below = lax.ppermute(
        state[:, :, 0:HALO, :], "rad", [(i + 1, i) for i in range(rad - 1)]
    )
    above = lax.ppermute(
        state[:, :, ROWS - HALO :, :], "rad", [(i, i + 1) for i in range(rad - 1)]
    )

    whole, edge = call(
        put_together, (f32(PLANES, TALL, LANES), f32(TALL, LANES)), [VMEM] * 3
    )(state, below, above)
    spin, drift, stiffness, shifts, edge = lax.optimization_barrier(
        (spin, drift, stiffness, shifts, edge)
    )
    edge = lax.ppermute(edge, "azi", [((i + 1) % azi, i) for i in range(azi)])

    rows = jnp.concatenate(
        [
            jnp.stack(
                [
                    NEAR - HD * drift,
                    NEAR + HD * drift,
                    (2.0 * DT) * spin,
                    (0.5 * DT) * spin,
                ]
            ),
            stiffness,
            jnp.ones((1, total), jnp.float32),
        ],
        axis=0,
    )
    rows = jnp.pad(rows, ((0, 0), (HALO, HALO)))
    near = lax.dynamic_slice_in_dim(rows, row_start, ROWS + 2 * HALO, axis=1)
    near = jnp.concatenate(
        [
            near[:, HALO:],
            jnp.zeros((rows.shape[0], TALL - ROWS - 2 * HALO), jnp.float32),
            near[:, :HALO],
        ],
        axis=1,
    )
    near = near.T

    own_row = row_start + 4 * (ring % 4) + ring // 4
    around = lax.dynamic_slice_in_dim(rows, own_row + REACH, 1 + HALO, axis=1).T
    turn = lax.dynamic_slice_in_dim(
        jnp.pad(shifts, (REACH, REACH)), own_row, 1 + HALO, axis=0
    )
    turn = jnp.concatenate([(turn + REACH) % (azi * LANES), turn[REACH : REACH + 1]])

    count = (4 + HALO) * PLANES
    tile = pltpu.VMEM((PLANES, TALL, 2 * LANES), jnp.float32)
    sent = call(
        first_step,
        f32(4, count, LANES),
        [VMEM] * 3,
        (
            tile,
            tile,
            tile,
            pltpu.VMEM((PACK * PLANES, LANES), jnp.float32),
            pltpu.VMEM((near.shape[1], TALL, LANES), jnp.float32),
        ),
    )(whole, edge, near)
    along_z = [[4 * x + z for z in range(4)] for x in range(4)]
    along_x = [[4 * x + z for x in range(4)] for z in range(4)]
    got = lax.all_to_all(sent, "azi", 0, 0, axis_index_groups=along_z)
    size = (1 + HALO) * PLANES
    sent = call(spread, f32(4, 4 * size, LANES), [VMEM])(got)
    got = lax.all_to_all(sent, "azi", 0, 0, axis_index_groups=along_x)
    band = pltpu.VMEM((1 + HALO, PLANES, 16, LANES), jnp.float32)
    sent = call(
        second_step, f32(16 * PACK, LANES), [SMEM, SMEM, VMEM], (band, band, band)
    )(turn, around, got.reshape(16 * size, LANES))
    got = lax.all_to_all(sent.reshape(16, PACK, LANES), "azi", 0, 0)
    return call(set_down, f32(FIELDS, LEVELS, ROWS, LANES), [VMEM])(
        got.reshape(16 * PACK, LANES)
    )


def solution(mesh):
    in_specs = (P(None, None, "rad", "azi"), P(), P(), P(), P())
    out_specs = P(None, None, "rad", "azi")
    return jax.shard_map(
        on_device, mesh=mesh, in_specs=in_specs, out_specs=out_specs, check_vma=False
    )
```

```python
import jax
import jax.numpy as jnp
from jax import lax
from jax.experimental import pallas as pl
from jax.experimental.pallas import tpu as pltpu
from jax.sharding import PartitionSpec as P

STEPS = 2
DT = 0.15
HD = 0.5 * DT
NEAR = DT * 0.05
SELF = 4.0 * DT * 0.05

FIELDS = 5
LEVELS = 4
PLANES = FIELDS * LEVELS
ROWS = 16
LANES = 128
REACH = 3
HALO = 2 * REACH
TALL = 32
PACK = 24
HELD = PLANES + 1
BAND = (1 + HALO) * HELD + 1
ROOM = 16 * 1024 * 1024


def cut(main_ref, low_ref, high_ref, kept_ref):
    for plane in range(PLANES):
        f, k = divmod(plane, LEVELS)
        low_ref[f, k] = main_ref[f, k, 0:HALO]
        high_ref[f, k] = main_ref[f, k, ROWS - HALO : ROWS]
        kept_ref[f, k] = main_ref[f, k]


def advance(at, slopes, coefs):
    a1, a2, twice, half, stiff = coefs
    rho, u, v, w, p = [slopes(f) for f in range(FIELDS)]
    w_up, w_down, p_up, p_down = at
    g = (u[1] - u[2]) + (v[3] - v[4])
    if w_up is not None:
        g = g + w_up
    if w_down is not None:
        g = g - w_down
    g = HD * g
    lift = 0.0
    if p_up is not None:
        lift = lift + p_up
    if p_down is not None:
        lift = lift - p_down
    own = [
        -g,
        twice * v[0] - HD * (p[1] - p[2]),
        -(half * u[0]) - HD * (p[3] - p[4]),
        -HD * lift,
        -(stiff * g),
    ]
    return [
        extra + ((a1 * q[3] + a2 * q[4]) + (NEAR * (q[1] + q[2]) - SELF * q[0]))
        for extra, q in zip(own, (rho, u, v, w, p))
    ]


def combine(stage, start, now, change):
    if stage == 0:
        return now + change
    if stage == 1:
        return 0.75 * start + 0.25 * (now + change)
    return start * (1.0 / 3.0) + (2.0 / 3.0) * (now + change)


def row_values(
    spin_hbm, drift_hbm, stiff_hbm, coef_ref, spin_ref, drift_ref, stiff_ref, sems
):
    copies = [
        pltpu.make_async_copy(source, target, sems.at[i])
        for i, (source, target) in enumerate(
            ((spin_hbm, spin_ref), (drift_hbm, drift_ref), (stiff_hbm, stiff_ref))
        )
    ]
    for copy in copies:
        copy.start()
    for copy in copies:
        copy.wait()
    wide = 2 * LANES
    total = spin_ref.shape[1]
    row_start = lax.axis_index("rad") * ROWS
    seen = lax.rem(row_start - HALO + total, total)
    here = pl.multiple_of(seen // LANES * LANES, LANES)
    after = pl.multiple_of(lax.rem(here + LANES, total), LANES)
    back = lax.rem(wide - lax.rem(seen, LANES), wide)

    def column(ref, i):
        pair = [ref[i : i + 1, pl.ds(start, LANES)] for start in (here, after)]
        pair = jnp.concatenate(pair, axis=1)
        pair = jnp.broadcast_to(pair, (8, wide))
        tall = jnp.transpose(pltpu.roll(pair, back, 1)[:, 0:LANES])[0:TALL]
        tall = pltpu.roll(tall, TALL - HALO, 0)
        return jnp.broadcast_to(tall[:, 0:1], (TALL, LANES))

    spin, drift = column(spin_ref, 0), column(drift_ref, 0)
    coef_ref[0] = NEAR - HD * drift
    coef_ref[1] = NEAR + HD * drift
    coef_ref[2] = (2.0 * DT) * spin
    coef_ref[3] = (0.5 * DT) * spin
    for k in range(LEVELS):
        coef_ref[4 + k] = column(stiff_ref, k)
    local = lax.broadcasted_iota(jnp.int32, (TALL, LANES), 0)
    local = row_start + jnp.where(local < ROWS + HALO, local, local - TALL)
    inside = (local >= 0) & (local < total)
    coef_ref[4 + LEVELS] = jnp.where(inside, 1.0, 0.0)


def first_step(
    main_ref,
    below_ref,
    above_ref,
    coef_ref,
    send_ref,
    begin,
    one,
    two,
    table,
):
    wide = 2 * LANES
    for plane in range(PLANES):
        f, k = divmod(plane, LEVELS)
        begin[plane, 0:ROWS, 0:LANES] = main_ref[f, k]
        begin[plane, ROWS : ROWS + HALO, 0:LANES] = below_ref[f, k]
        begin[plane, ROWS + HALO : TALL - HALO, 0:LANES] = jnp.zeros(
            (TALL - ROWS - 2 * HALO, LANES), jnp.float32
        )
        begin[plane, TALL - HALO : TALL, 0:LANES] = above_ref[f, k]
        begin[plane, :, LANES:wide] = jnp.zeros((TALL, LANES), jnp.float32)

    def coef(i):
        part = coef_ref[i]
        return jnp.concatenate([part, part], axis=1)

    sources = (begin, one, two)
    targets = (one, two, None)
    lane = lax.broadcasted_iota(jnp.int32, (TALL, LANES), 1)
    spill = jnp.zeros((TALL, LANES), jnp.float32)
    for stage in range(3):
        src, dst = sources[stage], targets[stage]
        for k in range(LEVELS):

            def slopes(f):
                c = src[f * LEVELS + k]
                return (
                    c,
                    pltpu.roll(c, TALL - 1, 0),
                    pltpu.roll(c, 1, 0),
                    pltpu.roll(c, wide - 1, 1),
                    pltpu.roll(c, 1, 1),
                )

            at = (
                src[3 * LEVELS + k + 1] if k + 1 < LEVELS else None,
                src[3 * LEVELS + k - 1] if k else None,
                src[4 * LEVELS + k + 1] if k + 1 < LEVELS else None,
                src[4 * LEVELS + k - 1] if k else None,
            )
            coefs = (coef(0), coef(1), coef(2), coef(3), coef(4 + k))
            valid = coef(4 + LEVELS) > 0.5
            change = advance(at, slopes, coefs)
            for f in range(FIELDS):
                plane = f * LEVELS + k
                value = combine(stage, begin[plane], src[plane], change[f])
                value = jnp.where(valid, value, 0.0)
                if dst is not None:
                    dst[plane] = value
                else:
                    table[pl.ds(plane, PACK, HELD), :] = pltpu.roll(
                        value[:, 0:LANES], REACH, 0
                    )[0:PACK]
                    past = pltpu.roll(
                        value[:, LANES:wide], (HALO * plane + REACH) % LANES, 1
                    )
                    mine = (lane >= HALO * plane) & (lane < HALO * (plane + 1))
                    spill = jnp.where(mine, past, spill)
    table[pl.ds(PLANES, PACK, HELD), :] = pltpu.roll(spill, REACH, 0)[0:PACK]
    size = (4 + HALO) * HELD
    for group in range(4):
        send_ref[group, 0:size, :] = table[group * 4 * HELD : group * 4 * HELD + size]
        send_ref[group, size:, :] = jnp.zeros(
            (send_ref.shape[1] - size, LANES), jnp.float32
        )


def spread(got_ref, send_ref):
    size = (1 + HALO) * HELD
    for target in range(4):
        for z in range(4):
            start = z * BAND
            send_ref[target, start : start + size, :] = got_ref[
                z, target * HELD : target * HELD + size, :
            ]
            send_ref[target, start + size : start + BAND, :] = jnp.zeros(
                (BAND - size, LANES), jnp.float32
            )


def turned(cells, amount, lane):
    blocks = amount // LANES
    offset = amount % LANES
    cells = pltpu.roll(cells, offset, 1)
    near = pltpu.roll(cells, blocks, 0)
    far = pltpu.roll(cells, lax.rem(blocks + 1, 16), 0)
    return jnp.where(lane >= offset, near, far)


def second_step(amount_ref, coef_ref, got_ref, send_ref, begin, one, two):
    lane = lax.broadcasted_iota(jnp.int32, (16, LANES), 1)
    edge = (lane < REACH) | (lane >= LANES - REACH)
    span = 1 + HALO
    for row in range(span):
        amount = amount_ref[row]
        spill = got_ref[pl.ds(row * HELD + PLANES, 16, BAND), :]
        spill = jnp.where(
            lax.rem(lane, HALO) < REACH,
            pltpu.roll(spill, 15, 0),
            pltpu.roll(spill, 1, 0),
        )
        for plane in range(PLANES):
            cells = got_ref[pl.ds(row * HELD + plane, 16, BAND), :]
            past = pltpu.roll(spill, LANES - REACH - HALO * plane, 1)
            cells = cells + jnp.where(edge, past, 0.0)
            begin[row, plane] = turned(cells, amount, lane)

    sources = (begin, one, two)
    targets = (one, two, None)
    last_amount = amount_ref[REACH]
    for stage in range(3):
        src, dst = sources[stage], targets[stage]
        for row in range(stage + 1, span - 1 - stage):
            scalars = [coef_ref[row, i] for i in range(5 + LEVELS)]
            for k in range(LEVELS):

                def slopes(f):
                    plane = f * LEVELS + k
                    c = src[row, plane]
                    ahead = pltpu.roll(c, LANES - 1, 1)
                    ahead = jnp.where(
                        lane == LANES - 1, pltpu.roll(ahead, 15, 0), ahead
                    )
                    behind = pltpu.roll(c, 1, 1)
                    behind = jnp.where(lane == 0, pltpu.roll(behind, 1, 0), behind)
                    return c, src[row + 1, plane], src[row - 1, plane], ahead, behind

                at = (
                    src[row, 3 * LEVELS + k + 1] if k + 1 < LEVELS else None,
                    src[row, 3 * LEVELS + k - 1] if k else None,
                    src[row, 4 * LEVELS + k + 1] if k + 1 < LEVELS else None,
                    src[row, 4 * LEVELS + k - 1] if k else None,
                )
                coefs = tuple(scalars[0:4]) + (scalars[4 + k],)
                change = advance(at, slopes, coefs)
                for f in range(FIELDS):
                    plane = f * LEVELS + k
                    value = combine(stage, begin[row, plane], src[row, plane], change[f])
                    if row != REACH:
                        value = jnp.where(scalars[4 + LEVELS] > 0.5, value, 0.0)
                    if dst is not None:
                        dst[row, plane] = value
                    else:
                        send_ref[pl.ds(plane, 16, PACK), :] = turned(
                            value, last_amount, lane
                        )
    for j in range(16):
        send_ref[j * PACK + PLANES : (j + 1) * PACK, :] = jnp.zeros(
            (PACK - PLANES, LANES), jnp.float32
        )


def set_down(got_ref, out_ref):
    for plane in range(PLANES):
        f, k = divmod(plane, LEVELS)
        for z in range(4):
            out_ref[f, k, 4 * z : 4 * z + 4, :] = got_ref[
                pl.ds(z * PACK + plane, 4, 4 * PACK), :
            ]


VMEM = pl.BlockSpec(memory_space=pltpu.VMEM)
SMEM = pl.BlockSpec(memory_space=pltpu.SMEM)


def f32(*shape):
    return jax.ShapeDtypeStruct(shape, jnp.float32)


def call(body, out_shape, in_specs, scratch=()):
    many = isinstance(out_shape, tuple)
    return pl.pallas_call(
        body,
        name=body.__name__,
        out_shape=out_shape,
        in_specs=in_specs,
        out_specs=(VMEM,) * len(out_shape) if many else VMEM,
        scratch_shapes=list(scratch),
        compiler_params=pltpu.CompilerParams(vmem_limit_bytes=ROOM),
    )


def on_device(state, shifts, spin, drift, stiffness):
    rad = lax.axis_size("rad")
    ring = lax.axis_index("azi")
    total = spin.shape[0]
    row_start = lax.axis_index("rad") * ROWS

    few = f32(FIELDS, LEVELS, HALO, LANES)
    low, high, state = call(cut, (few, few, f32(*state.shape)), [VMEM])(state)
    spin, drift, stiffness, low, high = lax.optimization_barrier(
        (spin, drift, stiffness, low, high)
    )
    coefs = call(
        row_values,
        f32(5 + LEVELS, TALL, LANES),
        [pl.BlockSpec(memory_space=pltpu.HBM)] * 3,
        (
            pltpu.VMEM((1, total), jnp.float32),
            pltpu.VMEM((1, total), jnp.float32),
            pltpu.VMEM((LEVELS, total), jnp.float32),
            pltpu.SemaphoreType.DMA((3,)),
        ),
    )(spin[None], drift[None], stiffness)
    below = lax.ppermute(low, "rad", [(i + 1, i) for i in range(rad - 1)])
    above = lax.ppermute(high, "rad", [(i, i + 1) for i in range(rad - 1)])

    count = (4 + HALO) * HELD
    count += -count % 8
    tile = pltpu.VMEM((PLANES, TALL, 2 * LANES), jnp.float32)
    sent = call(
        first_step,
        f32(4, count, LANES),
        [VMEM] * 4,
        (tile, tile, tile, pltpu.VMEM((PACK * HELD, LANES), jnp.float32)),
    )(state, below, above, coefs)
    along_z = [[4 * x + z for z in range(4)] for x in range(4)]
    along_x = [[4 * x + z for x in range(4)] for z in range(4)]
    got = lax.all_to_all(sent, "azi", 0, 0, axis_index_groups=along_z)
    sent = call(spread, f32(4, 4 * BAND, LANES), [VMEM])(got)

    spin, drift, stiffness, shifts, sent = lax.optimization_barrier(
        (spin, drift, stiffness, shifts, sent)
    )
    own_row = row_start + 4 * (ring % 4) + ring // 4
    rows = jnp.concatenate(
        [
            jnp.stack(
                [
                    NEAR - HD * drift,
                    NEAR + HD * drift,
                    (2.0 * DT) * spin,
                    (0.5 * DT) * spin,
                ]
            ),
            stiffness,
            jnp.ones((1, total), jnp.float32),
        ],
        axis=0,
    )
    rows = jnp.pad(rows, ((0, 0), (REACH, REACH)))
    around = lax.dynamic_slice_in_dim(rows, own_row, 1 + HALO, axis=1).T
    turn = lax.dynamic_slice_in_dim(
        jnp.pad(shifts, (REACH, REACH)), own_row, 1 + HALO, axis=0
    )

    got = lax.all_to_all(sent, "azi", 0, 0, axis_index_groups=along_x)
    band = pltpu.VMEM((1 + HALO, PLANES, 16, LANES), jnp.float32)
    sent = call(
        second_step, f32(16 * PACK, LANES), [SMEM, SMEM, VMEM], (band, band, band)
    )(turn, around, got.reshape(16 * BAND, LANES))
    got = lax.all_to_all(sent.reshape(16, PACK, LANES), "azi", 0, 0)
    return call(set_down, f32(FIELDS, LEVELS, ROWS, LANES), [VMEM])(
        got.reshape(16 * PACK, LANES)
    )


def solution(mesh):
    in_specs = (P(None, None, "rad", "azi"), P(), P(), P(), P())
    out_specs = P(None, None, "rad", "azi")
    return jax.shard_map(
        on_device, mesh=mesh, in_specs=in_specs, out_specs=out_specs, check_vma=False
    )
```

```python
import jax
import jax.numpy as jnp
from jax import lax
from jax.experimental import pallas as pl
from jax.experimental.pallas import tpu as pltpu
from jax.sharding import PartitionSpec as P

STEPS = 2
DT = 0.15
HD = 0.5 * DT
NEAR = DT * 0.05
SELF = 4.0 * DT * 0.05

FIELDS = 5
LEVELS = 4
PLANES = FIELDS * LEVELS
ROWS = 16
LANES = 128
REACH = 3
HALO = 2 * REACH
TALL = 32
PACK = 24
HELD = PLANES + 1
BAND = (1 + HALO) * HELD + 1
ROOM = 16 * 1024 * 1024


def cut(main_ref, low_ref, high_ref, kept_ref):
    for plane in range(PLANES):
        f, k = divmod(plane, LEVELS)
        low_ref[f, k] = main_ref[f, k, 0:HALO]
        high_ref[f, k] = main_ref[f, k, ROWS - HALO : ROWS]
        kept_ref[f, k] = main_ref[f, k]


def advance(at, slopes, coefs):
    a1, a2, twice, half, stiff = coefs
    rho, u, v, w, p = [slopes(f) for f in range(FIELDS)]
    w_up, w_down, p_up, p_down = at
    g = (u[1] - u[2]) + (v[3] - v[4])
    if w_up is not None:
        g = g + w_up
    if w_down is not None:
        g = g - w_down
    g = HD * g
    lift = 0.0
    if p_up is not None:
        lift = lift + p_up
    if p_down is not None:
        lift = lift - p_down
    own = [
        -g,
        twice * v[0] - HD * (p[1] - p[2]),
        -(half * u[0]) - HD * (p[3] - p[4]),
        -HD * lift,
        -(stiff * g),
    ]
    return [
        extra + ((a1 * q[3] + a2 * q[4]) + (NEAR * (q[1] + q[2]) - SELF * q[0]))
        for extra, q in zip(own, (rho, u, v, w, p))
    ]


def combine(stage, start, now, change):
    if stage == 0:
        return now + change
    if stage == 1:
        return 0.75 * start + 0.25 * (now + change)
    return start * (1.0 / 3.0) + (2.0 / 3.0) * (now + change)


def row_values(
    spin_hbm, drift_hbm, stiff_hbm, coef_ref, spin_ref, drift_ref, stiff_ref, sems
):
    copies = [
        pltpu.make_async_copy(source, target, sems.at[i])
        for i, (source, target) in enumerate(
            ((spin_hbm, spin_ref), (drift_hbm, drift_ref), (stiff_hbm, stiff_ref))
        )
    ]
    for copy in copies:
        copy.start()
    for copy in copies:
        copy.wait()
    wide = 2 * LANES
    total = spin_ref.shape[1]
    row_start = lax.axis_index("rad") * ROWS
    seen = lax.rem(row_start - HALO + total, total)
    here = pl.multiple_of(seen // LANES * LANES, LANES)
    after = pl.multiple_of(lax.rem(here + LANES, total), LANES)
    back = lax.rem(wide - lax.rem(seen, LANES), wide)

    def column(ref, i):
        pair = [ref[i : i + 1, pl.ds(start, LANES)] for start in (here, after)]
        pair = jnp.concatenate(pair, axis=1)
        pair = jnp.broadcast_to(pair, (8, wide))
        tall = jnp.transpose(pltpu.roll(pair, back, 1)[:, 0:LANES])[0:TALL]
        tall = pltpu.roll(tall, TALL - HALO, 0)
        return jnp.broadcast_to(tall[:, 0:1], (TALL, LANES))

    spin, drift = column(spin_ref, 0), column(drift_ref, 0)
    coef_ref[0] = NEAR - HD * drift
    coef_ref[1] = NEAR + HD * drift
    coef_ref[2] = (2.0 * DT) * spin
    coef_ref[3] = (0.5 * DT) * spin
    for k in range(LEVELS):
        coef_ref[4 + k] = column(stiff_ref, k)
    local = lax.broadcasted_iota(jnp.int32, (TALL, LANES), 0)
    local = row_start + jnp.where(local < ROWS + HALO, local, local - TALL)
    inside = (local >= 0) & (local < total)
    coef_ref[4 + LEVELS] = jnp.where(inside, 1.0, 0.0)


def first_step(
    main_ref,
    below_ref,
    above_ref,
    coef_ref,
    send_ref,
    begin,
    one,
    two,
    table,
):
    wide = 2 * LANES
    for plane in range(PLANES):
        f, k = divmod(plane, LEVELS)
        begin[plane, 0:ROWS, 0:LANES] = main_ref[f, k]
        begin[plane, ROWS : ROWS + HALO, 0:LANES] = below_ref[f, k]
        begin[plane, ROWS + HALO : TALL - HALO, 0:LANES] = jnp.zeros(
            (TALL - ROWS - 2 * HALO, LANES), jnp.float32
        )
        begin[plane, TALL - HALO : TALL, 0:LANES] = above_ref[f, k]
        begin[plane, :, LANES:wide] = jnp.zeros((TALL, LANES), jnp.float32)

    def coef(i):
        part = coef_ref[i]
        return jnp.concatenate([part, part], axis=1)

    sources = (begin, one, two)
    targets = (one, two, None)
    lane = lax.broadcasted_iota(jnp.int32, (TALL, LANES), 1)
    spill = jnp.zeros((TALL, LANES), jnp.float32)
    for stage in range(3):
        src, dst = sources[stage], targets[stage]
        for k in range(LEVELS):

            def slopes(f):
                c = src[f * LEVELS + k]
                return (
                    c,
                    pltpu.roll(c, TALL - 1, 0),
                    pltpu.roll(c, 1, 0),
                    pltpu.roll(c, wide - 1, 1),
                    pltpu.roll(c, 1, 1),
                )

            at = (
                src[3 * LEVELS + k + 1] if k + 1 < LEVELS else None,
                src[3 * LEVELS + k - 1] if k else None,
                src[4 * LEVELS + k + 1] if k + 1 < LEVELS else None,
                src[4 * LEVELS + k - 1] if k else None,
            )
            coefs = (coef(0), coef(1), coef(2), coef(3), coef(4 + k))
            valid = coef(4 + LEVELS) > 0.5
            change = advance(at, slopes, coefs)
            for f in range(FIELDS):
                plane = f * LEVELS + k
                value = combine(stage, begin[plane], src[plane], change[f])
                value = jnp.where(valid, value, 0.0)
                if dst is not None:
                    dst[plane] = value
                else:
                    table[pl.ds(plane, PACK, HELD), :] = pltpu.roll(
                        value[:, 0:LANES], REACH, 0
                    )[0:PACK]
                    past = pltpu.roll(
                        value[:, LANES:wide], (HALO * plane + REACH) % LANES, 1
                    )
                    mine = (lane >= HALO * plane) & (lane < HALO * (plane + 1))
                    spill = jnp.where(mine, past, spill)
    table[pl.ds(PLANES, PACK, HELD), :] = pltpu.roll(spill, REACH, 0)[0:PACK]
    size = (4 + HALO) * HELD
    for group in range(4):
        send_ref[group, 0:size, :] = table[group * 4 * HELD : group * 4 * HELD + size]
        send_ref[group, size:, :] = jnp.zeros(
            (send_ref.shape[1] - size, LANES), jnp.float32
        )


def spread(got_ref, send_ref):
    size = (1 + HALO) * HELD
    for target in range(4):
        for z in range(4):
            start = z * BAND
            send_ref[target, start : start + size, :] = got_ref[
                z, target * HELD : target * HELD + size, :
            ]
            send_ref[target, start + size : start + BAND, :] = jnp.zeros(
                (BAND - size, LANES), jnp.float32
            )


def turned(cells, amount, lane):
    blocks = amount // LANES
    offset = amount % LANES
    cells = pltpu.roll(cells, offset, 1)
    near = pltpu.roll(cells, blocks, 0)
    far = pltpu.roll(cells, lax.rem(blocks + 1, 16), 0)
    return jnp.where(lane >= offset, near, far)


def second_step(amount_ref, coef_ref, got_ref, send_ref, begin, one, two):
    lane = lax.broadcasted_iota(jnp.int32, (16, LANES), 1)
    edge = (lane < REACH) | (lane >= LANES - REACH)
    leftward = lax.rem(lane, HALO) < REACH
    span = 1 + HALO

    def take(row, carry):
        amount = amount_ref[row]
        first = row * HELD
        spill = got_ref[pl.ds(first + PLANES, 16, BAND), :]
        spill = jnp.where(
            leftward, pltpu.roll(spill, 15, 0), pltpu.roll(spill, 1, 0)
        )
        for plane in range(PLANES):
            cells = got_ref[pl.ds(first + plane, 16, BAND), :]
            past = pltpu.roll(spill, LANES - REACH - HALO * plane, 1)
            cells = cells + jnp.where(edge, past, 0.0)
            begin[row, plane] = turned(cells, amount, lane)
        return carry

    lax.fori_loop(0, span, take, 0)

    sources = (begin, one, two)
    targets = (one, two, None)
    last_amount = amount_ref[REACH]
    for stage in range(3):
        src, dst = sources[stage], targets[stage]

        def section(row, carry, stage=stage, src=src, dst=dst):
            scalars = [coef_ref[row, i] for i in range(5 + LEVELS)]
            inside = scalars[4 + LEVELS] > 0.5
            for k in range(LEVELS):

                def slopes(f):
                    plane = f * LEVELS + k
                    c = src[row, plane]
                    ahead = pltpu.roll(c, LANES - 1, 1)
                    ahead = jnp.where(
                        lane == LANES - 1, pltpu.roll(ahead, 15, 0), ahead
                    )
                    behind = pltpu.roll(c, 1, 1)
                    behind = jnp.where(lane == 0, pltpu.roll(behind, 1, 0), behind)
                    return c, src[row + 1, plane], src[row - 1, plane], ahead, behind

                at = (
                    src[row, 3 * LEVELS + k + 1] if k + 1 < LEVELS else None,
                    src[row, 3 * LEVELS + k - 1] if k else None,
                    src[row, 4 * LEVELS + k + 1] if k + 1 < LEVELS else None,
                    src[row, 4 * LEVELS + k - 1] if k else None,
                )
                coefs = tuple(scalars[0:4]) + (scalars[4 + k],)
                change = advance(at, slopes, coefs)
                for f in range(FIELDS):
                    plane = f * LEVELS + k
                    value = combine(stage, begin[row, plane], src[row, plane], change[f])
                    if dst is not None:
                        dst[row, plane] = jnp.where(inside, value, 0.0)
                    else:
                        send_ref[pl.ds(plane, 16, PLANES), :] = turned(
                            value, last_amount, lane
                        )
            return carry

        if dst is not None:
            lax.fori_loop(stage + 1, span - 1 - stage, section, 0)
        else:
            section(REACH, 0)


def set_down(got_ref, out_ref):
    for plane in range(PLANES):
        f, k = divmod(plane, LEVELS)
        for z in range(4):
            out_ref[f, k, 4 * z : 4 * z + 4, :] = got_ref[
                pl.ds(z * PLANES + plane, 4, 4 * PLANES), :
            ]


VMEM = pl.BlockSpec(memory_space=pltpu.VMEM)
SMEM = pl.BlockSpec(memory_space=pltpu.SMEM)


def f32(*shape):
    return jax.ShapeDtypeStruct(shape, jnp.float32)


def call(body, out_shape, in_specs, scratch=()):
    many = isinstance(out_shape, tuple)
    return pl.pallas_call(
        body,
        name=body.__name__,
        out_shape=out_shape,
        in_specs=in_specs,
        out_specs=(VMEM,) * len(out_shape) if many else VMEM,
        scratch_shapes=list(scratch),
        compiler_params=pltpu.CompilerParams(vmem_limit_bytes=ROOM),
    )


def on_device(state, shifts, spin, drift, stiffness):
    rad = lax.axis_size("rad")
    ring = lax.axis_index("azi")
    total = spin.shape[0]
    row_start = lax.axis_index("rad") * ROWS

    few = f32(FIELDS, LEVELS, HALO, LANES)
    low, high, state = call(cut, (few, few, f32(*state.shape)), [VMEM])(state)
    spin, drift, stiffness, low, high = lax.optimization_barrier(
        (spin, drift, stiffness, low, high)
    )
    coefs = call(
        row_values,
        f32(5 + LEVELS, TALL, LANES),
        [pl.BlockSpec(memory_space=pltpu.HBM)] * 3,
        (
            pltpu.VMEM((1, total), jnp.float32),
            pltpu.VMEM((1, total), jnp.float32),
            pltpu.VMEM((LEVELS, total), jnp.float32),
            pltpu.SemaphoreType.DMA((3,)),
        ),
    )(spin[None], drift[None], stiffness)
    below = lax.ppermute(low, "rad", [(i + 1, i) for i in range(rad - 1)])
    above = lax.ppermute(high, "rad", [(i, i + 1) for i in range(rad - 1)])

    count = (4 + HALO) * HELD
    count += -count % 8
    tile = pltpu.VMEM((PLANES, TALL, 2 * LANES), jnp.float32)
    sent = call(
        first_step,
        f32(4, count, LANES),
        [VMEM] * 4,
        (tile, tile, tile, pltpu.VMEM((PACK * HELD, LANES), jnp.float32)),
    )(state, below, above, coefs)
    along_z = [[4 * x + z for z in range(4)] for x in range(4)]
    along_x = [[4 * x + z for x in range(4)] for z in range(4)]
    got = lax.all_to_all(sent, "azi", 0, 0, axis_index_groups=along_z)
    sent = call(spread, f32(4, 4 * BAND, LANES), [VMEM])(got)

    spin, drift, stiffness, shifts, sent = lax.optimization_barrier(
        (spin, drift, stiffness, shifts, sent)
    )
    own_row = row_start + 4 * (ring % 4) + ring // 4
    rows = jnp.concatenate(
        [
            jnp.stack(
                [
                    NEAR - HD * drift,
                    NEAR + HD * drift,
                    (2.0 * DT) * spin,
                    (0.5 * DT) * spin,
                ]
            ),
            stiffness,
            jnp.ones((1, total), jnp.float32),
        ],
        axis=0,
    )
    rows = jnp.pad(rows, ((0, 0), (REACH, REACH)))
    around = lax.dynamic_slice_in_dim(rows, own_row, 1 + HALO, axis=1).T
    turn = lax.dynamic_slice_in_dim(
        jnp.pad(shifts, (REACH, REACH)), own_row, 1 + HALO, axis=0
    )

    got = lax.all_to_all(sent, "azi", 0, 0, axis_index_groups=along_x)
    band = pltpu.VMEM((1 + HALO, PLANES, 16, LANES), jnp.float32)
    sent = call(
        second_step, f32(16 * PLANES, LANES), [SMEM, SMEM, VMEM], (band, band, band)
    )(turn, around, got.reshape(16 * BAND, LANES))
    got = lax.all_to_all(sent.reshape(16, FIELDS, LEVELS, LANES), "azi", 0, 0)
    return call(set_down, f32(FIELDS, LEVELS, ROWS, LANES), [VMEM])(
        got.reshape(16 * PLANES, LANES)
    )


def solution(mesh):
    in_specs = (P(None, None, "rad", "azi"), P(), P(), P(), P())
    out_specs = P(None, None, "rad", "azi")
    return jax.shard_map(
        on_device, mesh=mesh, in_specs=in_specs, out_specs=out_specs, check_vma=False
    )
```

```python
import jax
import jax.numpy as jnp
from jax import lax
from jax.experimental import pallas as pl
from jax.experimental.pallas import tpu as pltpu
from jax.sharding import PartitionSpec as P

STEPS = 2
DT = 0.15
HD = 0.5 * DT
NEAR = DT * 0.05
SELF = 4.0 * DT * 0.05

FIELDS = 5
LEVELS = 4
PLANES = FIELDS * LEVELS
ROWS = 16
LANES = 128
REACH = 3
HALO = 2 * REACH
TALL = 32
PACK = 24
HELD = PLANES + 1
BAND = (1 + HALO) * HELD + 1
ROOM = 16 * 1024 * 1024


def cut(main_ref, low_ref, high_ref, kept_ref):
    for plane in range(PLANES):
        f, k = divmod(plane, LEVELS)
        low_ref[f, k] = main_ref[f, k, 0:HALO]
        high_ref[f, k] = main_ref[f, k, ROWS - HALO : ROWS]
        kept_ref[f, k] = main_ref[f, k]


def advance(at, slopes, coefs):
    a1, a2, twice, half, stiff = coefs
    rho, u, v, w, p = [slopes(f) for f in range(FIELDS)]
    w_up, w_down, p_up, p_down = at
    g = (u[1] - u[2]) + (v[3] - v[4])
    if w_up is not None:
        g = g + w_up
    if w_down is not None:
        g = g - w_down
    g = HD * g
    lift = 0.0
    if p_up is not None:
        lift = lift + p_up
    if p_down is not None:
        lift = lift - p_down
    own = [
        -g,
        twice * v[0] - HD * (p[1] - p[2]),
        -(half * u[0]) - HD * (p[3] - p[4]),
        -HD * lift,
        -(stiff * g),
    ]
    return [
        extra + ((a1 * q[3] + a2 * q[4]) + (NEAR * (q[1] + q[2]) - SELF * q[0]))
        for extra, q in zip(own, (rho, u, v, w, p))
    ]


def combine(stage, start, now, change):
    if stage == 0:
        return now + change
    if stage == 1:
        return 0.75 * start + 0.25 * (now + change)
    return start * (1.0 / 3.0) + (2.0 / 3.0) * (now + change)


def row_values(rows_ref, coef_ref):
    wide = 2 * LANES
    total = rows_ref.shape[1]
    row_start = lax.axis_index("rad") * ROWS
    seen = lax.rem(row_start - HALO + total, total)
    here = pl.multiple_of(seen // LANES * LANES, LANES)
    after = pl.multiple_of(lax.rem(here + LANES, total), LANES)
    back = lax.rem(wide - lax.rem(seen, LANES), wide)
    pair = [rows_ref[:, pl.ds(start, LANES)] for start in (here, after)]
    pair = pltpu.roll(jnp.concatenate(pair, axis=1), back, 1)
    tall = jnp.transpose(pair[:, 0:LANES])[0:TALL]
    tall = pltpu.roll(tall, TALL - HALO, 0)

    def column(i):
        return jnp.broadcast_to(tall[:, i : i + 1], (TALL, LANES))

    spin, drift = column(0), column(1)
    coef_ref[0] = NEAR - HD * drift
    coef_ref[1] = NEAR + HD * drift
    coef_ref[2] = (2.0 * DT) * spin
    coef_ref[3] = (0.5 * DT) * spin
    for k in range(LEVELS):
        coef_ref[4 + k] = column(2 + k)
    local = lax.broadcasted_iota(jnp.int32, (TALL, LANES), 0)
    local = row_start + jnp.where(local < ROWS + HALO, local, local - TALL)
    inside = (local >= 0) & (local < total)
    coef_ref[4 + LEVELS] = jnp.where(inside, 1.0, 0.0)


def first_step(
    main_ref,
    below_ref,
    above_ref,
    coef_ref,
    *rest,
):
    send_refs = rest[0:4]
    begin, one, two, table, ordered = rest[4:]
    wide = 2 * LANES
    for plane in range(PLANES):
        f, k = divmod(plane, LEVELS)
        begin[plane, 0:ROWS, 0:LANES] = main_ref[f, k]
        begin[plane, ROWS : ROWS + HALO, 0:LANES] = below_ref[f, k]
        begin[plane, ROWS + HALO : TALL - HALO, 0:LANES] = jnp.zeros(
            (TALL - ROWS - 2 * HALO, LANES), jnp.float32
        )
        begin[plane, TALL - HALO : TALL, 0:LANES] = above_ref[f, k]
        begin[plane, :, LANES:wide] = jnp.zeros((TALL, LANES), jnp.float32)

    def coef(i):
        part = coef_ref[i]
        return jnp.concatenate([part, part], axis=1)

    sources = (begin, one, two)
    targets = (one, two, None)
    lane = lax.broadcasted_iota(jnp.int32, (TALL, LANES), 1)
    spill = jnp.zeros((TALL, LANES), jnp.float32)
    for stage in range(3):
        src, dst = sources[stage], targets[stage]
        for k in range(LEVELS):

            def slopes(f):
                c = src[f * LEVELS + k]
                return (
                    c,
                    pltpu.roll(c, TALL - 1, 0),
                    pltpu.roll(c, 1, 0),
                    pltpu.roll(c, wide - 1, 1),
                    pltpu.roll(c, 1, 1),
                )

            at = (
                src[3 * LEVELS + k + 1] if k + 1 < LEVELS else None,
                src[3 * LEVELS + k - 1] if k else None,
                src[4 * LEVELS + k + 1] if k + 1 < LEVELS else None,
                src[4 * LEVELS + k - 1] if k else None,
            )
            coefs = (coef(0), coef(1), coef(2), coef(3), coef(4 + k))
            valid = coef(4 + LEVELS) > 0.5
            change = advance(at, slopes, coefs)
            for f in range(FIELDS):
                plane = f * LEVELS + k
                value = combine(stage, begin[plane], src[plane], change[f])
                value = jnp.where(valid, value, 0.0)
                if dst is not None:
                    dst[plane] = value
                else:
                    table[pl.ds(plane, PACK, HELD), :] = pltpu.roll(
                        value[:, 0:LANES], REACH, 0
                    )[0:PACK]
                    past = pltpu.roll(
                        value[:, LANES:wide], (HALO * plane + REACH) % LANES, 1
                    )
                    mine = (lane >= HALO * plane) & (lane < HALO * (plane + 1))
                    spill = jnp.where(mine, past, spill)
    table[pl.ds(PLANES, PACK, HELD), :] = pltpu.roll(spill, REACH, 0)[0:PACK]
    size = (4 + HALO) * HELD
    place = lax.axis_index("azi") % 4
    for group in range(4):
        ordered[group, 0:size, :] = table[group * 4 * HELD : group * 4 * HELD + size]
        ordered[group, size:, :] = jnp.zeros(
            (ordered.shape[1] - size, LANES), jnp.float32
        )
    for distance in range(4):
        send_refs[distance][...] = ordered[(place + distance) % 4]


def spread(*refs):
    got_refs, send_ref, ordered = refs[0:4], refs[4], refs[5]
    size = (1 + HALO) * HELD
    place = lax.axis_index("azi") % 4
    for distance in range(4):
        ordered[(place + 4 - distance) % 4] = got_refs[distance][...]
    for target in range(4):
        for z in range(4):
            start = z * BAND
            send_ref[target, start : start + size, :] = ordered[
                z, target * HELD : target * HELD + size, :
            ]
            send_ref[target, start + size : start + BAND, :] = jnp.zeros(
                (BAND - size, LANES), jnp.float32
            )


def turned(cells, amount, lane):
    blocks = amount // LANES
    offset = amount % LANES
    cells = pltpu.roll(cells, offset, 1)
    near = pltpu.roll(cells, blocks, 0)
    far = pltpu.roll(cells, lax.rem(blocks + 1, 16), 0)
    return jnp.where(lane >= offset, near, far)


def second_step(amount_ref, coef_ref, got_ref, send_ref, begin, one, two):
    lane = lax.broadcasted_iota(jnp.int32, (16, LANES), 1)
    edge = (lane < REACH) | (lane >= LANES - REACH)
    leftward = lax.rem(lane, HALO) < REACH
    span = 1 + HALO

    def take(row, carry):
        amount = amount_ref[row]
        first = row * HELD
        spill = got_ref[pl.ds(first + PLANES, 16, BAND), :]
        spill = jnp.where(
            leftward, pltpu.roll(spill, 15, 0), pltpu.roll(spill, 1, 0)
        )
        for plane in range(PLANES):
            cells = got_ref[pl.ds(first + plane, 16, BAND), :]
            past = pltpu.roll(spill, LANES - REACH - HALO * plane, 1)
            cells = cells + jnp.where(edge, past, 0.0)
            begin[row, plane] = turned(cells, amount, lane)
        return carry

    lax.fori_loop(0, span, take, 0)

    sources = (begin, one, two)
    targets = (one, two, None)
    last_amount = amount_ref[REACH]
    for stage in range(3):
        src, dst = sources[stage], targets[stage]

        def section(row, carry, stage=stage, src=src, dst=dst):
            scalars = [coef_ref[row, i] for i in range(5 + LEVELS)]
            inside = scalars[4 + LEVELS] > 0.5
            for k in range(LEVELS):

                def slopes(f):
                    plane = f * LEVELS + k
                    c = src[row, plane]
                    ahead = pltpu.roll(c, LANES - 1, 1)
                    ahead = jnp.where(
                        lane == LANES - 1, pltpu.roll(ahead, 15, 0), ahead
                    )
                    behind = pltpu.roll(c, 1, 1)
                    behind = jnp.where(lane == 0, pltpu.roll(behind, 1, 0), behind)
                    return c, src[row + 1, plane], src[row - 1, plane], ahead, behind

                at = (
                    src[row, 3 * LEVELS + k + 1] if k + 1 < LEVELS else None,
                    src[row, 3 * LEVELS + k - 1] if k else None,
                    src[row, 4 * LEVELS + k + 1] if k + 1 < LEVELS else None,
                    src[row, 4 * LEVELS + k - 1] if k else None,
                )
                coefs = tuple(scalars[0:4]) + (scalars[4 + k],)
                change = advance(at, slopes, coefs)
                for f in range(FIELDS):
                    plane = f * LEVELS + k
                    value = combine(stage, begin[row, plane], src[row, plane], change[f])
                    if dst is not None:
                        dst[row, plane] = jnp.where(inside, value, 0.0)
                    else:
                        send_ref[pl.ds(plane, 16, PLANES), :] = turned(
                            value, last_amount, lane
                        )
            return carry

        if dst is not None:
            lax.fori_loop(stage + 1, span - 1 - stage, section, 0)
        else:
            section(REACH, 0)


def set_down(got_ref, out_ref):
    for plane in range(PLANES):
        f, k = divmod(plane, LEVELS)
        for z in range(4):
            out_ref[f, k, 4 * z : 4 * z + 4, :] = got_ref[
                pl.ds(z * PLANES + plane, 4, 4 * PLANES), :
            ]


VMEM = pl.BlockSpec(memory_space=pltpu.VMEM)
SMEM = pl.BlockSpec(memory_space=pltpu.SMEM)


def f32(*shape):
    return jax.ShapeDtypeStruct(shape, jnp.float32)


def call(body, out_shape, in_specs, scratch=()):
    many = isinstance(out_shape, tuple)
    return pl.pallas_call(
        body,
        name=body.__name__,
        out_shape=out_shape,
        in_specs=in_specs,
        out_specs=(VMEM,) * len(out_shape) if many else VMEM,
        scratch_shapes=list(scratch),
        compiler_params=pltpu.CompilerParams(vmem_limit_bytes=ROOM),
    )


def on_device(state, shifts, spin, drift, stiffness):
    rad = lax.axis_size("rad")
    ring = lax.axis_index("azi")
    total = spin.shape[0]
    row_start = lax.axis_index("rad") * ROWS

    few = f32(FIELDS, LEVELS, HALO, LANES)
    low, high, state = call(cut, (few, few, f32(*state.shape)), [VMEM])(state)
    named = [spin[None], drift[None], stiffness]
    coefs = call(row_values, f32(5 + LEVELS, TALL, LANES), [VMEM])(
        jnp.concatenate(named + named[0:2], axis=0)
    )
    below = lax.ppermute(low, "rad", [(i + 1, i) for i in range(rad - 1)])
    above = lax.ppermute(high, "rad", [(i, i + 1) for i in range(rad - 1)])

    count = (4 + HALO) * HELD
    count += -count % 8
    tile = pltpu.VMEM((PLANES, TALL, 2 * LANES), jnp.float32)
    sent = call(
        first_step,
        (f32(count, LANES),) * 4,
        [VMEM] * 4,
        (
            tile,
            tile,
            tile,
            pltpu.VMEM((PACK * HELD, LANES), jnp.float32),
            pltpu.VMEM((4, count, LANES), jnp.float32),
        ),
    )(state, below, above, coefs)
    along_x = [[4 * x + z for x in range(4)] for z in range(4)]
    far, ahead, back = (
        lax.ppermute(
            sent[distance],
            "azi",
            [(4 * x + z, 4 * x + (z + distance) % 4) for x in range(4) for z in range(4)],
        )
        for distance in (2, 1, 3)
    )
    sent = call(
        spread,
        f32(4, 4 * BAND, LANES),
        [VMEM] * 4,
        (pltpu.VMEM((4, count, LANES), jnp.float32),),
    )(sent[0], ahead, far, back)

    spin, drift, stiffness, shifts, sent = lax.optimization_barrier(
        (spin, drift, stiffness, shifts, sent)
    )
    own_row = row_start + 4 * (ring % 4) + ring // 4
    rows = jnp.concatenate(
        [
            jnp.stack(
                [
                    NEAR - HD * drift,
                    NEAR + HD * drift,
                    (2.0 * DT) * spin,
                    (0.5 * DT) * spin,
                ]
            ),
            stiffness,
            jnp.ones((1, total), jnp.float32),
        ],
        axis=0,
    )
    rows = jnp.pad(rows, ((0, 0), (REACH, REACH)))
    around = lax.dynamic_slice_in_dim(rows, own_row, 1 + HALO, axis=1).T
    turn = lax.dynamic_slice_in_dim(
        jnp.pad(shifts, (REACH, REACH)), own_row, 1 + HALO, axis=0
    )

    got = lax.all_to_all(sent, "azi", 0, 0, axis_index_groups=along_x)
    band = pltpu.VMEM((1 + HALO, PLANES, 16, LANES), jnp.float32)
    sent = call(
        second_step, f32(16 * PLANES, LANES), [SMEM, SMEM, VMEM], (band, band, band)
    )(turn, around, got.reshape(16 * BAND, LANES))
    got = lax.all_to_all(sent.reshape(16, FIELDS, LEVELS, LANES), "azi", 0, 0)
    return call(set_down, f32(FIELDS, LEVELS, ROWS, LANES), [VMEM])(
        got.reshape(16 * PLANES, LANES)
    )


def solution(mesh):
    in_specs = (P(None, None, "rad", "azi"), P(), P(), P(), P())
    out_specs = P(None, None, "rad", "azi")
    return jax.shard_map(
        on_device, mesh=mesh, in_specs=in_specs, out_specs=out_specs, check_vma=False
    )
```

```python
import jax
import jax.numpy as jnp
from jax import lax
from jax.experimental import pallas as pl
from jax.experimental.pallas import tpu as pltpu
from jax.sharding import PartitionSpec as P

STEPS = 2
DT = 0.15
HD = 0.5 * DT
NEAR = DT * 0.05
SELF = 4.0 * DT * 0.05

FIELDS = 5
LEVELS = 4
PLANES = FIELDS * LEVELS
ROWS = 16
LANES = 128
REACH = 3
HALO = 2 * REACH
TALL = 32
PACK = 24
HELD = PLANES + 1
BAND = (1 + HALO) * HELD + 1
ROOM = 16 * 1024 * 1024


def cut(main_ref, low_ref, high_ref, kept_ref):
    for plane in range(PLANES):
        f, k = divmod(plane, LEVELS)
        low_ref[f, k] = main_ref[f, k, 0:HALO]
        high_ref[f, k] = main_ref[f, k, ROWS - HALO : ROWS]
        kept_ref[f, k] = main_ref[f, k]


def advance(at, slopes, coefs):
    a1, a2, twice, half, stiff = coefs
    rho, u, v, w, p = [slopes(f) for f in range(FIELDS)]
    w_up, w_down, p_up, p_down = at
    g = (u[1] - u[2]) + (v[3] - v[4])
    if w_up is not None:
        g = g + w_up
    if w_down is not None:
        g = g - w_down
    g = HD * g
    lift = 0.0
    if p_up is not None:
        lift = lift + p_up
    if p_down is not None:
        lift = lift - p_down
    own = [
        -g,
        twice * v[0] - HD * (p[1] - p[2]),
        -(half * u[0]) - HD * (p[3] - p[4]),
        -HD * lift,
        -(stiff * g),
    ]
    return [
        extra + ((a1 * q[3] + a2 * q[4]) + (NEAR * (q[1] + q[2]) - SELF * q[0]))
        for extra, q in zip(own, (rho, u, v, w, p))
    ]


def combine(stage, start, now, change):
    if stage == 0:
        return now + change
    if stage == 1:
        return 0.75 * start + 0.25 * (now + change)
    return start * (1.0 / 3.0) + (2.0 / 3.0) * (now + change)


def row_values(rows_ref, coef_ref):
    wide = 2 * LANES
    total = rows_ref.shape[1]
    row_start = lax.axis_index("rad") * ROWS
    seen = lax.rem(row_start - HALO + total, total)
    here = pl.multiple_of(seen // LANES * LANES, LANES)
    after = pl.multiple_of(lax.rem(here + LANES, total), LANES)
    back = lax.rem(wide - lax.rem(seen, LANES), wide)
    pair = [rows_ref[:, pl.ds(start, LANES)] for start in (here, after)]
    pair = pltpu.roll(jnp.concatenate(pair, axis=1), back, 1)
    tall = jnp.transpose(pair[:, 0:LANES])[0:TALL]
    tall = pltpu.roll(tall, TALL - HALO, 0)

    def column(i):
        return jnp.broadcast_to(tall[:, i : i + 1], (TALL, LANES))

    spin, drift = column(0), column(1)
    coef_ref[0] = NEAR - HD * drift
    coef_ref[1] = NEAR + HD * drift
    coef_ref[2] = (2.0 * DT) * spin
    coef_ref[3] = (0.5 * DT) * spin
    for k in range(LEVELS):
        coef_ref[4 + k] = column(2 + k)
    local = lax.broadcasted_iota(jnp.int32, (TALL, LANES), 0)
    local = row_start + jnp.where(local < ROWS + HALO, local, local - TALL)
    inside = (local >= 0) & (local < total)
    coef_ref[4 + LEVELS] = jnp.where(inside, 1.0, 0.0)


def first_step(
    main_ref,
    below_ref,
    above_ref,
    coef_ref,
    send_ref,
    begin,
    one,
    two,
    table,
):
    wide = 2 * LANES
    for plane in range(PLANES):
        f, k = divmod(plane, LEVELS)
        begin[plane, 0:ROWS, 0:LANES] = main_ref[f, k]
        begin[plane, ROWS : ROWS + HALO, 0:LANES] = below_ref[f, k]
        begin[plane, ROWS + HALO : TALL - HALO, 0:LANES] = jnp.zeros(
            (TALL - ROWS - 2 * HALO, LANES), jnp.float32
        )
        begin[plane, TALL - HALO : TALL, 0:LANES] = above_ref[f, k]
        begin[plane, :, LANES:wide] = jnp.zeros((TALL, LANES), jnp.float32)

    def coef(i):
        part = coef_ref[i]
        return jnp.concatenate([part, part], axis=1)

    sources = (begin, one, two)
    targets = (one, two, None)
    lane = lax.broadcasted_iota(jnp.int32, (TALL, LANES), 1)
    spill = jnp.zeros((TALL, LANES), jnp.float32)
    for stage in range(3):
        src, dst = sources[stage], targets[stage]
        for k in range(LEVELS):

            def slopes(f):
                c = src[f * LEVELS + k]
                return (
                    c,
                    pltpu.roll(c, TALL - 1, 0),
                    pltpu.roll(c, 1, 0),
                    pltpu.roll(c, wide - 1, 1),
                    pltpu.roll(c, 1, 1),
                )

            at = (
                src[3 * LEVELS + k + 1] if k + 1 < LEVELS else None,
                src[3 * LEVELS + k - 1] if k else None,
                src[4 * LEVELS + k + 1] if k + 1 < LEVELS else None,
                src[4 * LEVELS + k - 1] if k else None,
            )
            coefs = (coef(0), coef(1), coef(2), coef(3), coef(4 + k))
            valid = coef(4 + LEVELS) > 0.5
            change = advance(at, slopes, coefs)
            for f in range(FIELDS):
                plane = f * LEVELS + k
                value = combine(stage, begin[plane], src[plane], change[f])
                value = jnp.where(valid, value, 0.0)
                if dst is not None:
                    dst[plane] = value
                else:
                    table[pl.ds(plane, PACK, HELD), :] = pltpu.roll(
                        value[:, 0:LANES], REACH, 0
                    )[0:PACK]
                    past = pltpu.roll(
                        value[:, LANES:wide], (HALO * plane + REACH) % LANES, 1
                    )
                    mine = (lane >= HALO * plane) & (lane < HALO * (plane + 1))
                    spill = jnp.where(mine, past, spill)
    table[pl.ds(PLANES, PACK, HELD), :] = pltpu.roll(spill, REACH, 0)[0:PACK]
    size = (4 + HALO) * HELD
    for group in range(4):
        send_ref[group, 0:size, :] = table[group * 4 * HELD : group * 4 * HELD + size]
        send_ref[group, size:, :] = jnp.zeros(
            (send_ref.shape[1] - size, LANES), jnp.float32
        )


def spread(got_ref, send_ref):
    size = (1 + HALO) * HELD
    for target in range(4):
        for z in range(4):
            start = z * BAND
            send_ref[target, start : start + size, :] = got_ref[
                z, target * HELD : target * HELD + size, :
            ]
            send_ref[target, start + size : start + BAND, :] = jnp.zeros(
                (BAND - size, LANES), jnp.float32
            )


def turned(cells, amount, lane):
    blocks = amount // LANES
    offset = amount % LANES
    cells = pltpu.roll(cells, offset, 1)
    near = pltpu.roll(cells, blocks, 0)
    far = pltpu.roll(cells, lax.rem(blocks + 1, 16), 0)
    return jnp.where(lane >= offset, near, far)


def second_step(amount_ref, coef_ref, got_ref, send_ref, begin, one, two):
    lane = lax.broadcasted_iota(jnp.int32, (16, LANES), 1)
    edge = (lane < REACH) | (lane >= LANES - REACH)
    leftward = lax.rem(lane, HALO) < REACH
    span = 1 + HALO

    def take(row, carry):
        amount = amount_ref[row]
        first = row * HELD
        spill = got_ref[pl.ds(first + PLANES, 16, BAND), :]
        spill = jnp.where(
            leftward, pltpu.roll(spill, 15, 0), pltpu.roll(spill, 1, 0)
        )
        for plane in range(PLANES):
            cells = got_ref[pl.ds(first + plane, 16, BAND), :]
            past = pltpu.roll(spill, LANES - REACH - HALO * plane, 1)
            cells = cells + jnp.where(edge, past, 0.0)
            begin[row, plane] = turned(cells, amount, lane)
        return carry

    lax.fori_loop(0, span, take, 0)

    sources = (begin, one, two)
    targets = (one, two, None)
    last_amount = amount_ref[REACH]
    for stage in range(3):
        src, dst = sources[stage], targets[stage]

        def section(row):
            scalars = [coef_ref[row, i] for i in range(5 + LEVELS)]
            inside = scalars[4 + LEVELS] > 0.5
            for k in range(LEVELS):

                def slopes(f):
                    plane = f * LEVELS + k
                    c = src[row, plane]
                    ahead = pltpu.roll(c, LANES - 1, 1)
                    ahead = jnp.where(
                        lane == LANES - 1, pltpu.roll(ahead, 15, 0), ahead
                    )
                    behind = pltpu.roll(c, 1, 1)
                    behind = jnp.where(lane == 0, pltpu.roll(behind, 1, 0), behind)
                    return c, src[row + 1, plane], src[row - 1, plane], ahead, behind

                at = (
                    src[row, 3 * LEVELS + k + 1] if k + 1 < LEVELS else None,
                    src[row, 3 * LEVELS + k - 1] if k else None,
                    src[row, 4 * LEVELS + k + 1] if k + 1 < LEVELS else None,
                    src[row, 4 * LEVELS + k - 1] if k else None,
                )
                coefs = tuple(scalars[0:4]) + (scalars[4 + k],)
                change = advance(at, slopes, coefs)
                for f in range(FIELDS):
                    plane = f * LEVELS + k
                    value = combine(stage, begin[row, plane], src[row, plane], change[f])
                    if dst is not None:
                        if row != REACH:
                            value = jnp.where(inside, value, 0.0)
                        dst[row, plane] = value
                    else:
                        send_ref[pl.ds(plane, 16, PLANES), :] = turned(
                            value, last_amount, lane
                        )

        for row in range(stage + 1, span - 1 - stage):
            section(row)


def set_down(got_ref, out_ref):
    for plane in range(PLANES):
        f, k = divmod(plane, LEVELS)
        for z in range(4):
            out_ref[f, k, 4 * z : 4 * z + 4, :] = got_ref[
                pl.ds(z * PLANES + plane, 4, 4 * PLANES), :
            ]


VMEM = pl.BlockSpec(memory_space=pltpu.VMEM)
SMEM = pl.BlockSpec(memory_space=pltpu.SMEM)


def f32(*shape):
    return jax.ShapeDtypeStruct(shape, jnp.float32)


def call(body, out_shape, in_specs, scratch=()):
    many = isinstance(out_shape, tuple)
    return pl.pallas_call(
        body,
        name=body.__name__,
        out_shape=out_shape,
        in_specs=in_specs,
        out_specs=(VMEM,) * len(out_shape) if many else VMEM,
        scratch_shapes=list(scratch),
        compiler_params=pltpu.CompilerParams(vmem_limit_bytes=ROOM),
    )


def on_device(state, shifts, spin, drift, stiffness):
    rad = lax.axis_size("rad")
    ring = lax.axis_index("azi")
    total = spin.shape[0]
    row_start = lax.axis_index("rad") * ROWS

    few = f32(FIELDS, LEVELS, HALO, LANES)
    low, high, state = call(cut, (few, few, f32(*state.shape)), [VMEM])(state)
    named = [spin[None], drift[None], stiffness]
    coefs = call(row_values, f32(5 + LEVELS, TALL, LANES), [VMEM])(
        jnp.concatenate(named + named[0:2], axis=0)
    )
    below = lax.ppermute(low, "rad", [(i + 1, i) for i in range(rad - 1)])
    above = lax.ppermute(high, "rad", [(i, i + 1) for i in range(rad - 1)])

    count = (4 + HALO) * HELD
    count += -count % 8
    tile = pltpu.VMEM((PLANES, TALL, 2 * LANES), jnp.float32)
    sent = call(
        first_step,
        f32(4, count, LANES),
        [VMEM] * 4,
        (tile, tile, tile, pltpu.VMEM((PACK * HELD, LANES), jnp.float32)),
    )(state, below, above, coefs)
    along_z = [[4 * x + z for z in range(4)] for x in range(4)]
    along_x = [[4 * x + z for x in range(4)] for z in range(4)]
    got = lax.all_to_all(sent, "azi", 0, 0, axis_index_groups=along_z)
    sent = call(spread, f32(4, 4 * BAND, LANES), [VMEM])(got)

    spin, drift, stiffness, shifts, sent = lax.optimization_barrier(
        (spin, drift, stiffness, shifts, sent)
    )
    own_row = row_start + 4 * (ring % 4) + ring // 4
    rows = jnp.concatenate(
        [
            jnp.stack(
                [
                    NEAR - HD * drift,
                    NEAR + HD * drift,
                    (2.0 * DT) * spin,
                    (0.5 * DT) * spin,
                ]
            ),
            stiffness,
            jnp.ones((1, total), jnp.float32),
        ],
        axis=0,
    )
    rows = jnp.pad(rows, ((0, 0), (REACH, REACH)))
    around = lax.dynamic_slice_in_dim(rows, own_row, 1 + HALO, axis=1).T
    turn = lax.dynamic_slice_in_dim(
        jnp.pad(shifts, (REACH, REACH)), own_row, 1 + HALO, axis=0
    )

    got = lax.all_to_all(sent, "azi", 0, 0, axis_index_groups=along_x)
    band = pltpu.VMEM((1 + HALO, PLANES, 16, LANES), jnp.float32)
    sent = call(
        second_step, f32(16 * PLANES, LANES), [SMEM, SMEM, VMEM], (band, band, band)
    )(turn, around, got.reshape(16 * BAND, LANES))
    got = lax.all_to_all(sent.reshape(16, FIELDS, LEVELS, LANES), "azi", 0, 0)
    return call(set_down, f32(FIELDS, LEVELS, ROWS, LANES), [VMEM])(
        got.reshape(16 * PLANES, LANES)
    )


def solution(mesh):
    in_specs = (P(None, None, "rad", "azi"), P(), P(), P(), P())
    out_specs = P(None, None, "rad", "azi")
    return jax.shard_map(
        on_device, mesh=mesh, in_specs=in_specs, out_specs=out_specs, check_vma=False
    )
```

```python
import jax
import jax.numpy as jnp
from jax import lax
from jax.experimental import pallas as pl
from jax.experimental.pallas import tpu as pltpu
from jax.sharding import PartitionSpec as P

STEPS = 2
DT = 0.15
HD = 0.5 * DT
NEAR = DT * 0.05
SELF = 4.0 * DT * 0.05

FIELDS = 5
LEVELS = 4
PLANES = FIELDS * LEVELS
ROWS = 16
LANES = 128
REACH = 3
HALO = 2 * REACH
TALL = 32
PACK = 24
HELD = PLANES + 1
BAND = (1 + HALO) * HELD + 1
ROOM = 16 * 1024 * 1024


def cut(main_ref, low_ref, high_ref, kept_ref):
    for plane in range(PLANES):
        f, k = divmod(plane, LEVELS)
        low_ref[f, k] = main_ref[f, k, 0:HALO]
        high_ref[f, k] = main_ref[f, k, ROWS - HALO : ROWS]
        kept_ref[f, k] = main_ref[f, k]


def advance(at, slopes, coefs):
    a1, a2, twice, half, stiff = coefs
    rho, u, v, w, p = [slopes(f) for f in range(FIELDS)]
    w_up, w_down, p_up, p_down = at
    g = (u[1] - u[2]) + (v[3] - v[4])
    if w_up is not None:
        g = g + w_up
    if w_down is not None:
        g = g - w_down
    g = HD * g
    lift = 0.0
    if p_up is not None:
        lift = lift + p_up
    if p_down is not None:
        lift = lift - p_down
    own = [
        -g,
        twice * v[0] - HD * (p[1] - p[2]),
        -(half * u[0]) - HD * (p[3] - p[4]),
        -HD * lift,
        -(stiff * g),
    ]
    return [
        extra + ((a1 * q[3] + a2 * q[4]) + (NEAR * (q[1] + q[2]) - SELF * q[0]))
        for extra, q in zip(own, (rho, u, v, w, p))
    ]


def combine(stage, start, now, change):
    if stage == 0:
        return now + change
    if stage == 1:
        return 0.75 * start + 0.25 * (now + change)
    return start * (1.0 / 3.0) + (2.0 / 3.0) * (now + change)


def own_place():
    ring = lax.axis_index("azi")
    return 4 * (ring % 4) + ring // 4


def row_values(rows_ref, coef_ref, around_ref):
    wide = 2 * LANES
    total = rows_ref.shape[1]
    row_start = lax.axis_index("rad") * ROWS
    seen = lax.rem(row_start - HALO + total, total)
    here = pl.multiple_of(seen // LANES * LANES, LANES)
    after = pl.multiple_of(lax.rem(here + LANES, total), LANES)
    back = lax.rem(wide - lax.rem(seen, LANES), wide)
    pair = [rows_ref[:, pl.ds(start, LANES)] for start in (here, after)]
    pair = pltpu.roll(jnp.concatenate(pair, axis=1), back, 1)
    tall = jnp.transpose(pair[:, 0:LANES])[0:TALL]
    tall = pltpu.roll(tall, TALL - HALO, 0)

    def column(i):
        return jnp.broadcast_to(tall[:, i : i + 1], (TALL, LANES))

    spin, drift = column(0), column(1)
    coef_ref[0] = NEAR - HD * drift
    coef_ref[1] = NEAR + HD * drift
    coef_ref[2] = (2.0 * DT) * spin
    coef_ref[3] = (0.5 * DT) * spin
    for k in range(LEVELS):
        coef_ref[4 + k] = column(2 + k)
    local = lax.broadcasted_iota(jnp.int32, (TALL, LANES), 0)
    local = row_start + jnp.where(local < ROWS + HALO, local, local - TALL)
    inside = (local >= 0) & (local < total)
    coef_ref[4 + LEVELS] = jnp.where(inside, 1.0, 0.0)
    turn = lax.rem(TALL + REACH - own_place(), TALL)
    for i in range(5 + LEVELS):
        around_ref[i] = pltpu.roll(coef_ref[i], turn, 0)[0:8]


def first_step(
    main_ref,
    below_ref,
    above_ref,
    coef_ref,
    send_ref,
    begin,
    one,
    two,
    table,
):
    wide = 2 * LANES
    for plane in range(PLANES):
        f, k = divmod(plane, LEVELS)
        begin[plane, 0:ROWS, 0:LANES] = main_ref[f, k]
        begin[plane, ROWS : ROWS + HALO, 0:LANES] = below_ref[f, k]
        begin[plane, ROWS + HALO : TALL - HALO, 0:LANES] = jnp.zeros(
            (TALL - ROWS - 2 * HALO, LANES), jnp.float32
        )
        begin[plane, TALL - HALO : TALL, 0:LANES] = above_ref[f, k]
        begin[plane, :, LANES:wide] = jnp.zeros((TALL, LANES), jnp.float32)

    def coef(i):
        part = coef_ref[i]
        return jnp.concatenate([part, part], axis=1)

    sources = (begin, one, two)
    targets = (one, two, None)
    lane = lax.broadcasted_iota(jnp.int32, (TALL, LANES), 1)
    spill = jnp.zeros((TALL, LANES), jnp.float32)
    for stage in range(3):
        src, dst = sources[stage], targets[stage]
        for k in range(LEVELS):

            def slopes(f):
                c = src[f * LEVELS + k]
                return (
                    c,
                    pltpu.roll(c, TALL - 1, 0),
                    pltpu.roll(c, 1, 0),
                    pltpu.roll(c, wide - 1, 1),
                    pltpu.roll(c, 1, 1),
                )

            at = (
                src[3 * LEVELS + k + 1] if k + 1 < LEVELS else None,
                src[3 * LEVELS + k - 1] if k else None,
                src[4 * LEVELS + k + 1] if k + 1 < LEVELS else None,
                src[4 * LEVELS + k - 1] if k else None,
            )
            coefs = (coef(0), coef(1), coef(2), coef(3), coef(4 + k))
            valid = coef(4 + LEVELS) > 0.5
            change = advance(at, slopes, coefs)
            for f in range(FIELDS):
                plane = f * LEVELS + k
                value = combine(stage, begin[plane], src[plane], change[f])
                value = jnp.where(valid, value, 0.0)
                if dst is not None:
                    dst[plane] = value
                else:
                    table[pl.ds(plane, PACK, HELD), :] = pltpu.roll(
                        value[:, 0:LANES], REACH, 0
                    )[0:PACK]
                    past = pltpu.roll(
                        value[:, LANES:wide], (HALO * plane + REACH) % LANES, 1
                    )
                    mine = (lane >= HALO * plane) & (lane < HALO * (plane + 1))
                    spill = jnp.where(mine, past, spill)
    table[pl.ds(PLANES, PACK, HELD), :] = pltpu.roll(spill, REACH, 0)[0:PACK]
    size = (4 + HALO) * HELD
    for group in range(4):
        send_ref[group, 0:size, :] = table[group * 4 * HELD : group * 4 * HELD + size]
        send_ref[group, size:, :] = jnp.zeros(
            (send_ref.shape[1] - size, LANES), jnp.float32
        )


def spread(got_ref, send_ref):
    size = (1 + HALO) * HELD
    for target in range(4):
        for z in range(4):
            start = z * BAND
            send_ref[target, start : start + size, :] = got_ref[
                z, target * HELD : target * HELD + size, :
            ]
            send_ref[target, start + size : start + BAND, :] = jnp.zeros(
                (BAND - size, LANES), jnp.float32
            )


def turned(cells, amount, lane):
    blocks = amount // LANES
    offset = amount % LANES
    cells = pltpu.roll(cells, offset, 1)
    near = pltpu.roll(cells, blocks, 0)
    far = pltpu.roll(cells, lax.rem(blocks + 1, 16), 0)
    return jnp.where(lane >= offset, near, far)


def second_step(shift_ref, coef_ref, got_ref, send_ref, begin, one, two):
    lane = lax.broadcasted_iota(jnp.int32, (16, LANES), 1)
    edge = (lane < REACH) | (lane >= LANES - REACH)
    leftward = lax.rem(lane, HALO) < REACH
    span = 1 + HALO
    own_row = lax.axis_index("rad") * ROWS + own_place()
    last = shift_ref.shape[0] - 1

    def take(row, carry):
        amount = shift_ref[jnp.clip(own_row - REACH + row, 0, last)]
        first = row * HELD
        spill = got_ref[pl.ds(first + PLANES, 16, BAND), :]
        spill = jnp.where(
            leftward, pltpu.roll(spill, 15, 0), pltpu.roll(spill, 1, 0)
        )
        for plane in range(PLANES):
            cells = got_ref[pl.ds(first + plane, 16, BAND), :]
            past = pltpu.roll(spill, LANES - REACH - HALO * plane, 1)
            cells = cells + jnp.where(edge, past, 0.0)
            begin[row, plane] = turned(cells, amount, lane)
        return carry

    lax.fori_loop(0, span, take, 0)

    sources = (begin, one, two)
    targets = (one, two, None)
    last_amount = shift_ref[own_row]
    for stage in range(3):
        src, dst = sources[stage], targets[stage]

        def section(row):
            scalars = [
                jnp.broadcast_to(coef_ref[i, row : row + 1, :], (16, LANES))
                for i in range(5 + LEVELS)
            ]
            inside = scalars[4 + LEVELS] > 0.5
            for k in range(LEVELS):

                def slopes(f):
                    plane = f * LEVELS + k
                    c = src[row, plane]
                    ahead = pltpu.roll(c, LANES - 1, 1)
                    ahead = jnp.where(
                        lane == LANES - 1, pltpu.roll(ahead, 15, 0), ahead
                    )
                    behind = pltpu.roll(c, 1, 1)
                    behind = jnp.where(lane == 0, pltpu.roll(behind, 1, 0), behind)
                    return c, src[row + 1, plane], src[row - 1, plane], ahead, behind

                at = (
                    src[row, 3 * LEVELS + k + 1] if k + 1 < LEVELS else None,
                    src[row, 3 * LEVELS + k - 1] if k else None,
                    src[row, 4 * LEVELS + k + 1] if k + 1 < LEVELS else None,
                    src[row, 4 * LEVELS + k - 1] if k else None,
                )
                coefs = tuple(scalars[0:4]) + (scalars[4 + k],)
                change = advance(at, slopes, coefs)
                for f in range(FIELDS):
                    plane = f * LEVELS + k
                    value = combine(stage, begin[row, plane], src[row, plane], change[f])
                    if dst is not None:
                        if row != REACH:
                            value = jnp.where(inside, value, 0.0)
                        dst[row, plane] = value
                    else:
                        send_ref[pl.ds(plane, 16, PLANES), :] = turned(
                            value, last_amount, lane
                        )

        for row in range(stage + 1, span - 1 - stage):
            section(row)


def set_down(got_ref, out_ref):
    for plane in range(PLANES):
        f, k = divmod(plane, LEVELS)
        for z in range(4):
            out_ref[f, k, 4 * z : 4 * z + 4, :] = got_ref[
                pl.ds(z * PLANES + plane, 4, 4 * PLANES), :
            ]


VMEM = pl.BlockSpec(memory_space=pltpu.VMEM)
SMEM = pl.BlockSpec(memory_space=pltpu.SMEM)


def f32(*shape):
    return jax.ShapeDtypeStruct(shape, jnp.float32)


def call(body, out_shape, in_specs, scratch=()):
    many = isinstance(out_shape, tuple)
    return pl.pallas_call(
        body,
        name=body.__name__,
        out_shape=out_shape,
        in_specs=in_specs,
        out_specs=(VMEM,) * len(out_shape) if many else VMEM,
        scratch_shapes=list(scratch),
        compiler_params=pltpu.CompilerParams(vmem_limit_bytes=ROOM),
    )


def on_device(state, shifts, spin, drift, stiffness):
    rad = lax.axis_size("rad")
    few = f32(FIELDS, LEVELS, HALO, LANES)
    low, high, state = call(cut, (few, few, f32(*state.shape)), [VMEM])(state)
    named = [spin[None], drift[None], stiffness]
    coefs, around = call(
        row_values,
        (f32(5 + LEVELS, TALL, LANES), f32(5 + LEVELS, 8, LANES)),
        [VMEM],
    )(
        jnp.concatenate(named + named[0:2], axis=0)
    )
    below = lax.ppermute(low, "rad", [(i + 1, i) for i in range(rad - 1)])
    above = lax.ppermute(high, "rad", [(i, i + 1) for i in range(rad - 1)])

    count = (4 + HALO) * HELD
    count += -count % 8
    tile = pltpu.VMEM((PLANES, TALL, 2 * LANES), jnp.float32)
    sent = call(
        first_step,
        f32(4, count, LANES),
        [VMEM] * 4,
        (tile, tile, tile, pltpu.VMEM((PACK * HELD, LANES), jnp.float32)),
    )(state, below, above, coefs)
    along_z = [[4 * x + z for z in range(4)] for x in range(4)]
    along_x = [[4 * x + z for x in range(4)] for z in range(4)]
    got = lax.all_to_all(sent, "azi", 0, 0, axis_index_groups=along_z)
    sent = call(spread, f32(4, 4 * BAND, LANES), [VMEM])(got)

    got = lax.all_to_all(sent, "azi", 0, 0, axis_index_groups=along_x)
    band = pltpu.VMEM((1 + HALO, PLANES, 16, LANES), jnp.float32)
    sent = call(
        second_step, f32(16 * PLANES, LANES), [SMEM, VMEM, VMEM], (band, band, band)
    )(shifts, around, got.reshape(16 * BAND, LANES))
    got = lax.all_to_all(sent.reshape(16, FIELDS, LEVELS, LANES), "azi", 0, 0)
    return call(set_down, f32(FIELDS, LEVELS, ROWS, LANES), [VMEM])(
        got.reshape(16 * PLANES, LANES)
    )


def solution(mesh):
    in_specs = (P(None, None, "rad", "azi"), P(), P(), P(), P())
    out_specs = P(None, None, "rad", "azi")
    return jax.shard_map(
        on_device, mesh=mesh, in_specs=in_specs, out_specs=out_specs, check_vma=False
    )
```

```python
import jax
import jax.numpy as jnp
from jax import lax
from jax.experimental import pallas as pl
from jax.experimental.pallas import tpu as pltpu
from jax.sharding import PartitionSpec as P

STEPS = 2
DT = 0.15
HD = 0.5 * DT
NEAR = DT * 0.05
SELF = 4.0 * DT * 0.05

FIELDS = 5
LEVELS = 4
PLANES = FIELDS * LEVELS
ROWS = 16
LANES = 128
REACH = 3
HALO = 2 * REACH
TALL = 32
PACK = 24
HELD = PLANES + 1
BAND = (1 + HALO) * HELD + 1
ROOM = 16 * 1024 * 1024


def cut(main_ref, high_ref, low_ref, kept_ref):
    for plane in range(PLANES):
        f, k = divmod(plane, LEVELS)
        low_ref[f, k] = main_ref[f, k, 0:HALO]
        high_ref[f, k] = main_ref[f, k, ROWS - HALO : ROWS]
        kept_ref[f, k] = main_ref[f, k]


def advance(at, slopes, coefs):
    a1, a2, twice, half, stiff = coefs
    rho, u, v, w, p = [slopes(f) for f in range(FIELDS)]
    w_up, w_down, p_up, p_down = at
    g = (u[1] - u[2]) + (v[3] - v[4])
    if w_up is not None:
        g = g + w_up
    if w_down is not None:
        g = g - w_down
    g = HD * g
    lift = 0.0
    if p_up is not None:
        lift = lift + p_up
    if p_down is not None:
        lift = lift - p_down
    own = [
        -g,
        twice * v[0] - HD * (p[1] - p[2]),
        -(half * u[0]) - HD * (p[3] - p[4]),
        -HD * lift,
        -(stiff * g),
    ]
    return [
        extra + ((a1 * q[3] + a2 * q[4]) + (NEAR * (q[1] + q[2]) - SELF * q[0]))
        for extra, q in zip(own, (rho, u, v, w, p))
    ]


def combine(stage, start, now, change):
    if stage == 0:
        return now + change
    if stage == 1:
        return 0.75 * start + 0.25 * (now + change)
    return start * (1.0 / 3.0) + (2.0 / 3.0) * (now + change)


def own_place():
    ring = lax.axis_index("azi")
    return 4 * (ring % 4) + ring // 4


def row_values(rows_ref, coef_ref, around_ref):
    wide = 2 * LANES
    total = rows_ref.shape[1]
    row_start = lax.axis_index("rad") * ROWS
    seen = lax.rem(row_start - HALO + total, total)
    here = pl.multiple_of(seen // LANES * LANES, LANES)
    after = pl.multiple_of(lax.rem(here + LANES, total), LANES)
    back = lax.rem(wide - lax.rem(seen, LANES), wide)
    pair = [rows_ref[:, pl.ds(start, LANES)] for start in (here, after)]
    pair = pltpu.roll(jnp.concatenate(pair, axis=1), back, 1)
    tall = jnp.transpose(pair[:, 0:LANES])[0:TALL]
    tall = pltpu.roll(tall, TALL - HALO, 0)

    def column(i):
        return jnp.broadcast_to(tall[:, i : i + 1], (TALL, LANES))

    spin, drift = column(0), column(1)
    coef_ref[0] = NEAR - HD * drift
    coef_ref[1] = NEAR + HD * drift
    coef_ref[2] = (2.0 * DT) * spin
    coef_ref[3] = (0.5 * DT) * spin
    for k in range(LEVELS):
        coef_ref[4 + k] = column(2 + k)
    local = lax.broadcasted_iota(jnp.int32, (TALL, LANES), 0)
    local = row_start + jnp.where(local < ROWS + HALO, local, local - TALL)
    inside = (local >= 0) & (local < total)
    coef_ref[4 + LEVELS] = jnp.where(inside, 1.0, 0.0)
    turn = lax.rem(TALL + REACH - own_place(), TALL)
    for i in range(5 + LEVELS):
        around_ref[i] = pltpu.roll(coef_ref[i], turn, 0)[0:8]


def first_step(
    main_ref,
    above_ref,
    below_ref,
    coef_ref,
    send_ref,
    begin,
    one,
    two,
    table,
):
    wide = 2 * LANES
    for plane in range(PLANES):
        f, k = divmod(plane, LEVELS)
        begin[plane, 0:ROWS, 0:LANES] = main_ref[f, k]
        begin[plane, ROWS : ROWS + HALO, 0:LANES] = below_ref[f, k]
        begin[plane, ROWS + HALO : TALL - HALO, 0:LANES] = jnp.zeros(
            (TALL - ROWS - 2 * HALO, LANES), jnp.float32
        )
        begin[plane, TALL - HALO : TALL, 0:LANES] = above_ref[f, k]
        begin[plane, :, LANES:wide] = jnp.zeros((TALL, LANES), jnp.float32)

    def coef(i):
        part = coef_ref[i]
        return jnp.concatenate([part, part], axis=1)

    sources = (begin, one, two)
    targets = (one, two, None)
    lane = lax.broadcasted_iota(jnp.int32, (TALL, LANES), 1)
    spill = jnp.zeros((TALL, LANES), jnp.float32)
    for stage in range(3):
        src, dst = sources[stage], targets[stage]
        for k in range(LEVELS):

            def slopes(f):
                c = src[f * LEVELS + k]
                return (
                    c,
                    pltpu.roll(c, TALL - 1, 0),
                    pltpu.roll(c, 1, 0),
                    pltpu.roll(c, wide - 1, 1),
                    pltpu.roll(c, 1, 1),
                )

            at = (
                src[3 * LEVELS + k + 1] if k + 1 < LEVELS else None,
                src[3 * LEVELS + k - 1] if k else None,
                src[4 * LEVELS + k + 1] if k + 1 < LEVELS else None,
                src[4 * LEVELS + k - 1] if k else None,
            )
            coefs = (coef(0), coef(1), coef(2), coef(3), coef(4 + k))
            valid = coef(4 + LEVELS) > 0.5
            change = advance(at, slopes, coefs)
            for f in range(FIELDS):
                plane = f * LEVELS + k
                value = combine(stage, begin[plane], src[plane], change[f])
                value = jnp.where(valid, value, 0.0)
                if dst is not None:
                    dst[plane] = value
                else:
                    table[pl.ds(plane, PACK, HELD), :] = pltpu.roll(
                        value[:, 0:LANES], REACH, 0
                    )[0:PACK]
                    past = pltpu.roll(
                        value[:, LANES:wide], (HALO * plane + REACH) % LANES, 1
                    )
                    mine = (lane >= HALO * plane) & (lane < HALO * (plane + 1))
                    spill = jnp.where(mine, past, spill)
    table[pl.ds(PLANES, PACK, HELD), :] = pltpu.roll(spill, REACH, 0)[0:PACK]
    size = (4 + HALO) * HELD
    for group in range(4):
        send_ref[group, 0:size, :] = table[group * 4 * HELD : group * 4 * HELD + size]
        send_ref[group, size:, :] = jnp.zeros(
            (send_ref.shape[1] - size, LANES), jnp.float32
        )


def spread(got_ref, send_ref):
    size = (1 + HALO) * HELD
    for target in range(4):
        for z in range(4):
            start = z * BAND
            send_ref[target, start : start + size, :] = got_ref[
                z, target * HELD : target * HELD + size, :
            ]
            send_ref[target, start + size : start + BAND, :] = jnp.zeros(
                (BAND - size, LANES), jnp.float32
            )


def turned(cells, amount, lane):
    blocks = amount // LANES
    offset = amount % LANES
    cells = pltpu.roll(cells, offset, 1)
    near = pltpu.roll(cells, blocks, 0)
    far = pltpu.roll(cells, lax.rem(blocks + 1, 16), 0)
    return jnp.where(lane >= offset, near, far)


def second_step(shift_ref, coef_ref, got_ref, send_ref, begin, one, two):
    lane = lax.broadcasted_iota(jnp.int32, (16, LANES), 1)
    edge = (lane < REACH) | (lane >= LANES - REACH)
    leftward = lax.rem(lane, HALO) < REACH
    span = 1 + HALO
    own_row = lax.axis_index("rad") * ROWS + own_place()
    last = shift_ref.shape[0] - 1

    def take(row, carry):
        amount = shift_ref[jnp.clip(own_row - REACH + row, 0, last)]
        first = row * HELD
        spill = got_ref[pl.ds(first + PLANES, 16, BAND), :]
        spill = jnp.where(
            leftward, pltpu.roll(spill, 15, 0), pltpu.roll(spill, 1, 0)
        )
        for plane in range(PLANES):
            cells = got_ref[pl.ds(first + plane, 16, BAND), :]
            past = pltpu.roll(spill, LANES - REACH - HALO * plane, 1)
            cells = cells + jnp.where(edge, past, 0.0)
            begin[row, plane] = turned(cells, amount, lane)
        return carry

    lax.fori_loop(0, span, take, 0)

    sources = (begin, one, two)
    targets = (one, two, None)
    last_amount = shift_ref[own_row]
    for stage in range(3):
        src, dst = sources[stage], targets[stage]

        def section(row):
            scalars = [
                jnp.broadcast_to(coef_ref[i, row : row + 1, :], (16, LANES))
                for i in range(5 + LEVELS)
            ]
            inside = scalars[4 + LEVELS] > 0.5
            for k in range(LEVELS):

                def slopes(f):
                    plane = f * LEVELS + k
                    c = src[row, plane]
                    ahead = pltpu.roll(c, LANES - 1, 1)
                    ahead = jnp.where(
                        lane == LANES - 1, pltpu.roll(ahead, 15, 0), ahead
                    )
                    behind = pltpu.roll(c, 1, 1)
                    behind = jnp.where(lane == 0, pltpu.roll(behind, 1, 0), behind)
                    return c, src[row + 1, plane], src[row - 1, plane], ahead, behind

                at = (
                    src[row, 3 * LEVELS + k + 1] if k + 1 < LEVELS else None,
                    src[row, 3 * LEVELS + k - 1] if k else None,
                    src[row, 4 * LEVELS + k + 1] if k + 1 < LEVELS else None,
                    src[row, 4 * LEVELS + k - 1] if k else None,
                )
                coefs = tuple(scalars[0:4]) + (scalars[4 + k],)
                change = advance(at, slopes, coefs)
                for f in range(FIELDS):
                    plane = f * LEVELS + k
                    value = combine(stage, begin[row, plane], src[row, plane], change[f])
                    if dst is not None:
                        if row != REACH:
                            value = jnp.where(inside, value, 0.0)
                        dst[row, plane] = value
                    else:
                        send_ref[pl.ds(plane, 16, PLANES), :] = turned(
                            value, last_amount, lane
                        )

        for row in range(stage + 1, span - 1 - stage):
            section(row)


def set_down(got_ref, out_ref):
    for plane in range(PLANES):
        f, k = divmod(plane, LEVELS)
        for z in range(4):
            out_ref[f, k, 4 * z : 4 * z + 4, :] = got_ref[
                pl.ds(z * PLANES + plane, 4, 4 * PLANES), :
            ]


VMEM = pl.BlockSpec(memory_space=pltpu.VMEM)
SMEM = pl.BlockSpec(memory_space=pltpu.SMEM)


def f32(*shape):
    return jax.ShapeDtypeStruct(shape, jnp.float32)


def call(body, out_shape, in_specs, scratch=()):
    many = isinstance(out_shape, tuple)
    return pl.pallas_call(
        body,
        name=body.__name__,
        out_shape=out_shape,
        in_specs=in_specs,
        out_specs=(VMEM,) * len(out_shape) if many else VMEM,
        scratch_shapes=list(scratch),
        compiler_params=pltpu.CompilerParams(vmem_limit_bytes=ROOM),
    )


def on_device(state, shifts, spin, drift, stiffness):
    rad = lax.axis_size("rad")
    few = f32(FIELDS, LEVELS, HALO, LANES)
    high, low, state = call(cut, (few, few, f32(*state.shape)), [VMEM])(state)
    named = [spin[None], drift[None], stiffness]
    coefs, around = call(
        row_values,
        (f32(5 + LEVELS, TALL, LANES), f32(5 + LEVELS, 8, LANES)),
        [VMEM],
    )(
        jnp.concatenate(named + named[0:2], axis=0)
    )
    above = lax.ppermute(high, "rad", [(i, i + 1) for i in range(rad - 1)])
    below = lax.ppermute(low, "rad", [(i + 1, i) for i in range(rad - 1)])

    count = (4 + HALO) * HELD
    count += -count % 8
    tile = pltpu.VMEM((PLANES, TALL, 2 * LANES), jnp.float32)
    sent = call(
        first_step,
        f32(4, count, LANES),
        [VMEM] * 4,
        (tile, tile, tile, pltpu.VMEM((PACK * HELD, LANES), jnp.float32)),
    )(state, above, below, coefs)
    along_z = [[4 * x + z for z in range(4)] for x in range(4)]
    along_x = [[4 * x + z for x in range(4)] for z in range(4)]
    got = lax.all_to_all(sent, "azi", 0, 0, axis_index_groups=along_z)
    sent = call(spread, f32(4, 4 * BAND, LANES), [VMEM])(got)

    got = lax.all_to_all(sent, "azi", 0, 0, axis_index_groups=along_x)
    band = pltpu.VMEM((1 + HALO, PLANES, 16, LANES), jnp.float32)
    sent = call(
        second_step, f32(16 * PLANES, LANES), [SMEM, VMEM, VMEM], (band, band, band)
    )(shifts, around, got.reshape(16 * BAND, LANES))
    got = lax.all_to_all(sent.reshape(16, FIELDS, LEVELS, LANES), "azi", 0, 0)
    return call(set_down, f32(FIELDS, LEVELS, ROWS, LANES), [VMEM])(
        got.reshape(16 * PLANES, LANES)
    )


def solution(mesh):
    in_specs = (P(None, None, "rad", "azi"), P(), P(), P(), P())
    out_specs = P(None, None, "rad", "azi")
    return jax.shard_map(
        on_device, mesh=mesh, in_specs=in_specs, out_specs=out_specs, check_vma=False
    )
```
